32 devices in a mesh: wide: 4 (over y, x), narrow: 8 (over z, core).
Axes of the slice: x: 2, y: 2, z: 4, core: 2. Of those that a mesh axis runs over, the one named last changes fastest.
Arguments:
- positions: float32 [384, 3, 256], P(('wide', 'narrow')), may hold values from 6 to 18
- forces: float32 [384, 256], P(('wide', 'narrow')), may hold values from -0.6 to 0.6
- counts: int32 [384], P(('wide', 'narrow')), may hold values from 0 to 256, as said below
- anchors: int32 [3, 384], P(None, ('wide', 'narrow')), may hold values from 0 to 1023, as said below
- helpers: int32 [384, 1], P(('wide', 'narrow')), may hold values from 0 to 7, as said below
Outputs:
- spectrum: float32 [2, 32, 1024, 1024], P(None, 'wide', 'narrow')
- helper_load: float32 [4, 8], P('wide', 'narrow')
The draws below stay inside these ranges and needn't reach their ends.
Inputs may be any that keep to these rules, and one draw needn't show every extreme that they name: `counts`: within each device's 12 bins the bins with a nonzero count come first; some device has all its bins nonzero. `helpers`: within each device's 12 bins at most 2 bins name the same helper. anchors[0] < 8, anchors[1] < 128, anchors[2] < 1024.
All inputs are finite; a program needn't handle non-finite values.
Results may differ from the reference program's by a relative error of at most 0.0054.
Values may be sent and summed in bfloat16 or wider, within the bound.
A program may use at most 128 MiB of HBM per device.

```python
import math
import jax
import jax.numpy as jnp
from jax import lax

XS = 8
NY = 1024
NZ = 1024
PATCH = 24
BIN = 256
BINS_DEV = 12
BINS = 384
N_WIDE = 4
N_NARROW = 8
DEVICES = 32


def draw_positions(key, part):
    first_key, second_key, third_key = jax.random.split(key, 3)
    lowest = float(PATCH // 4)
    topmost = float(3 * PATCH // 4)
    array_dims = (BINS_DEV * DEVICES, 3, BIN)
    scattered = jax.random.uniform(first_key, array_dims, jnp.float32, lowest, topmost)
    chooser = jax.random.randint(second_key, array_dims, 0, 8)
    sided = jax.random.randint(third_key, array_dims, 0, 2)
    at_ends = jnp.where(sided == 0, jnp.float32(lowest), jnp.float32(topmost))
    end_share = 2
    return jnp.where(chooser < end_share, at_ends, scattered).astype(jnp.float32)


def draw_counts(key, part):
    first_key, second_key, third_key = jax.random.split(key, 3)
    level = jax.random.randint(first_key, (DEVICES,), 0, 8)
    living = jnp.maximum(1, BINS_DEV * level ** 3 // 343)
    filled = jax.random.randint(second_key, (), 0, DEVICES)
    living = jnp.where(jnp.arange(DEVICES) == filled, BINS_DEV, living)
    ordinal = jnp.arange(BINS_DEV)
    alive = ordinal[None, :] < living[:, None]
    sizes = jax.random.randint(third_key, (DEVICES, BINS_DEV), 1, BIN + 1)
    return jnp.where(alive, sizes, 0).reshape(-1).astype(jnp.int32)


def draw_anchors(key, part):
    limits = jnp.array([XS, NY // N_NARROW, NZ], jnp.int32)
    return jax.random.randint(key, (3, BINS_DEV * DEVICES), 0, limits[:, None]).astype(jnp.int32)


def draw_helpers(key, part):
    device_keys = jax.random.split(key, DEVICES)
    slot_total = N_NARROW * ((BINS_DEV + N_NARROW - 1) // N_NARROW)
    shuffled = jax.vmap(lambda single: jax.random.permutation(single, slot_total))(device_keys)
    chosen = shuffled[:, :BINS_DEV] // ((BINS_DEV + N_NARROW - 1) // N_NARROW)
    return chosen.reshape(BINS_DEV * DEVICES, 1).astype(jnp.int32)


def steps_of(key, dims, pieces, least, largest):
    gain, own = 1.0, jax.random.fold_in(key, 6)
    for dim, blocks in pieces:
        steps = jnp.exp(jax.random.uniform(jax.random.fold_in(own, dim), (blocks,), jnp.float32, least / len(pieces), largest / len(pieces)))
        gain = gain * jnp.repeat(steps, dims[dim] // blocks).reshape([-1 if axis == dim else 1 for axis in range(len(dims))])
    return gain


def centred(key, shape, scale, limit, pieces=(), kind=jnp.bfloat16):
    entries = jax.random.normal(key, shape, jnp.float32) * scale
    if len(pieces) > 0:
        entries = steps_of(key, shape, pieces, -0.22, 0.18) * entries
    return jnp.clip(entries, min=-limit, max=limit).astype(kind)


def setup_inputs(seed: int = 0) -> dict:
    key_list = jax.random.split(jax.random.key(seed), 6)
    positions = draw_positions(jax.random.fold_in(key_list[5], 71), 0)
    forces = centred(key_list[1], (BINS, BIN), 0.1, 0.6, ((0, 32),), jnp.float32)
    counts = draw_counts(jax.random.fold_in(key_list[5], 71), 0)
    anchors = draw_anchors(jax.random.fold_in(key_list[5], 71), 0)
    helpers = draw_helpers(jax.random.fold_in(key_list[5], 71), 0)
    return dict(positions=positions, forces=forces, counts=counts, anchors=anchors, helpers=helpers)


spread_rate = 0.08
two_pi = 2.0 * math.pi

def bin_patch(places, strength, number):
    cell_index = jnp.arange(PATCH, dtype=jnp.float32)
    living = jnp.arange(BIN, dtype=jnp.int32) < number
    weights = jnp.where(living, strength, jnp.zeros_like(strength))
    along_x = jnp.exp(-spread_rate * (cell_index[None, :] - places[0][:, None]) ** 2)
    along_y = jnp.exp(-spread_rate * (cell_index[None, :] - places[1][:, None]) ** 2)
    along_z = jnp.exp(-spread_rate * (cell_index[None, :] - places[2][:, None]) ** 2)
    left_side = weights[:, None] * along_x
    right_side = (along_y[:, :, None] * along_z[:, None, :]).reshape(BIN, PATCH * PATCH)
    return jnp.dot(left_side.T, right_side, precision=lax.Precision.HIGHEST)

def unchanged(volume):
    return volume

def dft_tables(length, columns):
    ordinal = jnp.arange(length, dtype=jnp.int32)
    phase = ordinal[:, None] * columns[None, :] % length
    angle = phase.astype(jnp.float32) * (two_pi / length)
    norm_scale = 1.0 / math.sqrt(length)
    return ((jnp.cos(angle) * norm_scale).astype(jnp.bfloat16), (jnp.sin(angle) * norm_scale).astype(jnp.bfloat16))

def reference(positions, forces, counts, anchors, helpers):
    width_x = XS * N_WIDE
    own_rows = NY // N_NARROW
    total_bins = BINS_DEV * N_WIDE * N_NARROW
    padded = jnp.zeros((width_x + PATCH, NY + PATCH, NZ + PATCH), jnp.float32)

    def place(bin_index, padded):
        bin_index = jnp.asarray(bin_index).astype(jnp.int32)
        device = bin_index // BINS_DEV
        corner = (device // N_NARROW * XS + anchors[0, bin_index], device % N_NARROW * own_rows + anchors[1, bin_index], anchors[2, bin_index])
        corner = tuple((entry.astype(jnp.int32) for entry in corner))

        def added(volume):
            patch = bin_patch(positions[bin_index], forces[bin_index], counts[bin_index])
            rounded = lax.optimization_barrier(patch.astype(jnp.bfloat16)).astype(jnp.float32)
            rounded = rounded.reshape(PATCH, PATCH, PATCH)
            region = lax.dynamic_slice(volume, corner, (PATCH, PATCH, PATCH))
            return lax.dynamic_update_slice(volume, region + rounded, corner)
        return lax.cond(counts[bin_index] > 0, added, unchanged, padded)
    padded = lax.fori_loop(0, total_bins, place, padded)
    folded = padded[:width_x].at[:PATCH].add(padded[width_x:])
    folded = folded[:, :NY].at[:, :PATCH].add(folded[:, NY:])
    folded = folded[:, :, :NZ].at[:, :, :PATCH].add(folded[:, :, NZ:])
    block_rows = NZ // N_NARROW
    slot_index = jnp.arange(NZ, dtype=jnp.int32)
    column_order = (slot_index % block_rows * N_NARROW + slot_index // block_rows).astype(jnp.int32)
    cos_z, sin_z = dft_tables(NZ, column_order)
    cos_y, sin_y = dft_tables(NY, jnp.arange(NY, dtype=jnp.int32))

    def transform(plane):
        half = plane.astype(jnp.bfloat16)
        z_real = jnp.dot(half, cos_z, preferred_element_type=jnp.float32).astype(jnp.bfloat16)
        z_imag = (-jnp.dot(half, sin_z, preferred_element_type=jnp.float32)).astype(jnp.bfloat16)
        out_real = jnp.dot(z_real.T, cos_y, preferred_element_type=jnp.float32) + jnp.dot(z_imag.T, sin_y, preferred_element_type=jnp.float32)
        out_imag = jnp.dot(z_imag.T, cos_y, preferred_element_type=jnp.float32) - jnp.dot(z_real.T, sin_y, preferred_element_type=jnp.float32)
        return jnp.stack([out_real, out_imag])
    spectra = lax.map(transform, folded)
    spectrum = jnp.moveaxis(spectra, 1, 0).astype(jnp.float32)
    group_help = helpers.reshape(N_WIDE, BINS_DEV * N_NARROW)
    group_count = counts.reshape(N_WIDE, BINS_DEV * N_NARROW).astype(jnp.float32)
    matches = group_help[:, :, None] == jnp.arange(N_NARROW, dtype=jnp.int32)[None, None, :]
    helper_load = lax.optimization_barrier(jnp.sum(jnp.where(matches, group_count[:, :, None], jnp.zeros_like(group_count)[:, :, None]), axis=1)) / BIN
    return (spectrum, helper_load.astype(jnp.float32))
```

```python
import math

import jax
import jax.numpy as jnp
import numpy as np
from jax import lax
from jax.experimental import pallas as pl
from jax.experimental.pallas import tpu as pltpu
from jax.sharding import PartitionSpec as P

XS = 8
NY = 1024
NZ = 1024
PATCH = 24
SPLIT = 8
WINDOW = 32
TOGETHER = 2
LANES = 128
PAIR = 2

LOWEST, SPAN = 6.0, 12.0
POSITION_STEPS = 65535.0
FORCE_STEPS = 32000.0
FORCE_ZERO = 32768

spread_rate = 0.08
spread_root = math.sqrt(spread_rate / math.log(2.0))
two_pi = 2.0 * math.pi


def y_tables():
    points = NY // SPLIT
    y = np.arange(points)[None, :] * SPLIT + np.arange(SPLIT)[:, None]
    phase = (y[:, :, None] * np.arange(points)[None, None, :]) % NY
    angle = phase * (two_pi / NY)
    cos = np.cos(angle) / math.sqrt(NY)
    sin = np.sin(angle) / math.sqrt(NY)
    upper = np.concatenate([cos, -sin], axis=2)
    lower = np.concatenate([sin, cos], axis=2)
    return np.concatenate([upper, lower], axis=1).astype(np.float32).astype(jnp.bfloat16)


def z_tables(block, count):
    frequency = np.arange(block)[None, :] * count + np.arange(count)[:, None]
    phase = frequency[:, :, None] * np.arange(block)[None, None, :] % NZ
    angle = phase * (two_pi / NZ)
    cos = np.cos(angle) / math.sqrt(NZ)
    sin = np.sin(angle) / math.sqrt(NZ)
    top = np.concatenate([cos, sin], axis=2)
    bottom = np.concatenate([-sin, cos], axis=2)
    return np.concatenate([top, bottom], axis=1).astype(np.float32).astype(jnp.bfloat16)


def turns(count):
    angle = np.arange(count) * (two_pi / count)
    return np.concatenate([np.cos(angle), -np.sin(angle)]).astype(np.float32)


def encode(positions, forces, counts, anchors, helpers, own, bins):
    particles = forces.shape[1]
    scale = POSITION_STEPS / SPAN

    def place(c):
        code = (positions[:, c, :] - LOWEST) * scale + 0.5
        return jnp.clip(code, 0.0, POSITION_STEPS).astype(jnp.int32)

    lane = lax.broadcasted_iota(jnp.int32, (bins, LANES), 1)
    bin_of = lax.broadcasted_iota(jnp.int32, (bins, LANES), 0)
    row = jnp.concatenate(
        [
            counts[...],
            anchors[0:1, :],
            anchors[1:2, :],
            anchors[2:3, :],
            helpers[...],
            jnp.zeros((1, LANES - 5 * bins), jnp.int32),
        ],
        axis=1,
    )
    spread_counts = jnp.broadcast_to(row.astype(jnp.float32), (bins, LANES))
    live = jnp.sum(jnp.where(lane == bin_of, spread_counts, 0.0), axis=1, keepdims=True)
    slot = lax.broadcasted_iota(jnp.int32, (bins, particles), 1).astype(jnp.float32)
    force = jnp.where(slot < live, forces[...], 0.0)
    largest = jnp.max(jnp.max(jnp.abs(force), axis=1, keepdims=True), axis=0, keepdims=True)
    power = jnp.ceil(jnp.log2(jnp.maximum(largest, 1e-36)))
    code = (force * jnp.exp2(-power) * FORCE_STEPS + (FORCE_ZERO + 0.5)).astype(jnp.int32)
    first = lax.shift_left(place(0), 16) | place(1)
    second = lax.shift_left(place(2), 16) | code
    for h in range(particles // LANES):
        own[h * bins : (h + 1) * bins, :] = first[:, h * LANES : (h + 1) * LANES]
    for h in range(particles // LANES):
        at = particles // LANES * bins + h * bins
        own[at : at + bins, :] = second[:, h * LANES : (h + 1) * LANES]
    at = 2 * particles // LANES * bins
    lane = lax.broadcasted_iota(jnp.int32, (1, LANES), 1)
    power = jnp.broadcast_to(power.astype(jnp.int32), (1, LANES))
    alive = jnp.where((lane < bins) & (row > 0), 1.0, 0.0)
    alive = jnp.sum(alive, axis=1, keepdims=True).astype(jnp.int32)
    row = jnp.where(lane == 5 * bins, power, row)
    own[at : at + 1, :] = jnp.where(lane == 5 * bins + 1, alive, row)


def gather_kernel(
    positions, forces, counts, anchors, helpers, parts, own, send, receive, local,
    *, wide, count, slabs, stride
):
    w, n = lax.axis_index("wide"), lax.axis_index("narrow")
    chips = count // 2
    z, core = n // 2, n % 2
    other = z * 2 + (1 - core)

    def place(distance, index):
        return parts.at[distance * count + index]

    def at(distance, index):
        return receive.at[distance * count + index]

    def later(distance):
        return (w + distance) % wide

    peers = [((z + step) % chips) * 2 + core for step in range(1, chips)]
    barrier = pltpu.get_barrier_semaphore()
    for peer in peers + [other]:
        pl.semaphore_signal(
            barrier, inc=1, device_id=(w, peer), device_id_type=pl.DeviceIdType.MESH
        )
    for distance in range(1, slabs):
        pl.semaphore_signal(
            barrier,
            inc=1,
            device_id=((w + wide - distance) % wide, n),
            device_id_type=pl.DeviceIdType.MESH,
        )
    encode(positions, forces, counts, anchors, helpers, own, forces.shape[0])
    pl.semaphore_wait(barrier, chips + slabs - 1)

    sent = []

    def push(source, target, distance, index):
        copy = pltpu.make_async_remote_copy(
            src_ref=source,
            dst_ref=place(distance, index),
            send_sem=send.at[len(sent)],
            recv_sem=at(distance, index),
            device_id=target,
            device_id_type=pl.DeviceIdType.MESH,
        )
        copy.start()
        sent.append(copy)

    def arrived(distance, index):
        pltpu.make_async_remote_copy(
            src_ref=own,
            dst_ref=place(distance, index),
            send_sem=send.at[0],
            recv_sem=at(distance, index),
            device_id=(w, other),
            device_id_type=pl.DeviceIdType.MESH,
        ).wait_recv()

    for peer in peers:
        push(own, (w, peer), 0, n)
    for distance in range(1, slabs):
        push(own, (later(distance), n), distance, n)
    push(own, (w, other), 0, n)
    keep = pltpu.make_async_copy(own, place(0, n), local)
    keep.start()
    sources = [((z + chips - step) % chips) * 2 + core for step in range(chips)]
    for source in sources[1:]:
        arrived(0, source)
        for distance in range(1, slabs):
            push(place(0, source), (later(distance), n), distance, source)
        push(place(0, source), (w, other), 0, source)
    for source in sources:
        for distance in range(1, slabs):
            arrived(distance, source)
            push(place(distance, source), (w, other), distance, source)
    for distance in range(slabs):
        for chip in range(chips):
            arrived(distance, chip * 2 + (1 - core))
    for copy in sent:
        copy.wait_send()
    keep.wait()


def spectrum_kernel(
    turn, parts_hbm, ztab_hbm, ytab_hbm, out, load, folded, facts, coded, upper, lower, items,
    ztab, ytab, terms, results, lefts, rights, sems, sent,
    *, bins, block, count, own_rows, slabs
):
    me = lax.axis_index("narrow")
    slots = slabs * count
    halves = lefts.shape[2] // LANES
    particles = halves * LANES
    half_rows = halves * bins
    meta = 2 * half_rows
    folds = 2 * block // LANES
    pitch = NY + WINDOW
    points = NY // SPLIT

    to_smem = pltpu.make_async_copy(parts_hbm.at[:, meta, :], facts, sems.at[0])
    to_vmem = pltpu.make_async_copy(parts_hbm, coded, sems.at[1])
    z_copy = pltpu.make_async_copy(ztab_hbm.at[me], ztab, sems.at[2])
    y_copy = pltpu.make_async_copy(ytab_hbm, ytab, sems.at[3])
    to_smem.start()
    to_vmem.start()
    z_copy.start()
    y_copy.start()
    to_smem.wait()
    to_vmem.wait()

    home = jnp.concatenate([coded[d, meta : meta + 1, :] for d in range(count)], axis=0)
    helper = pltpu.roll(home, LANES - 4 * bins, axis=1)
    lane = lax.broadcasted_iota(jnp.int32, home.shape, 1)
    mine = jnp.where((lane < bins) & (helper == me), home, 0).astype(jnp.float32)
    load[...] = jnp.sum(mine, keepdims=True).reshape(1, 1) / particles

    zero_rows = XS * pitch * folds // slots

    def per_device(device, total):
        flat = pl.multiple_of(device * zero_rows, 8)
        folded[pl.ds(flat, zero_rows), :] = jnp.zeros((zero_rows, LANES), jnp.float32)
        alive = facts[device, 5 * bins + 1]
        power = facts[device, 5 * bins].astype(jnp.float32)
        for b in range(bins):
            items[total + b] = device * 16 + b
        gain = jnp.exp2(jnp.full((1, LANES), power)) * (1.0 / FORCE_STEPS)
        word = coded[device, :meta, :]
        high = lax.shift_right_logical(word, 16).astype(jnp.float32)
        low = (word & 65535).astype(jnp.float32)
        unit = SPAN / POSITION_STEPS * spread_root
        upper[pl.ds(pl.multiple_of(device * meta, 8), meta), :] = high * unit + LOWEST * spread_root
        lower[pl.ds(pl.multiple_of(device * meta, 8), half_rows), :] = (
            low[:half_rows] * unit + LOWEST * spread_root
        )
        lower[pl.ds(pl.multiple_of(device * meta + half_rows, 8), half_rows), :] = (
            low[half_rows:] - FORCE_ZERO
        ) * gain
        return total + alive

    total = lax.fori_loop(0, slots, per_device, 0)
    for extra in range(4 * TOGETHER):
        items[total + extra] = 0

    cell = lax.broadcasted_iota(jnp.int32, (8, particles), 0)
    steps8 = cell.astype(jnp.float32) * spread_root

    def gauss(first, place):
        away = (steps8 + first * spread_root) - place
        return jnp.exp2(-(away * away))

    def line(ref, row):
        return jnp.concatenate([ref[pl.ds(row + h * bins, 1), :] for h in range(halves)], axis=1)

    def build(k, left, right):
        item = items[k]
        device, b = item // 16, item % 16
        r = device * meta + b
        x0 = device // count * XS - facts[device, bins + b]
        y0 = facts[device, 2 * bins + b]
        px = line(upper, r) - x0.astype(jnp.float32) * spread_root
        pz = line(upper, r + half_rows)
        force = line(lower, r + half_rows)
        force = jnp.where(k < total, force, jnp.zeros_like(force))
        along_x = gauss(0, px) * force
        along_x = jnp.where((cell >= -x0) & (cell < PATCH - x0), along_x, 0.0)
        shift = y0 & 7
        py = line(lower, r) + shift.astype(jnp.float32) * spread_root
        along_y = [gauss(8 * i, py) for i in range(4)]
        along_y[0] = jnp.where(cell >= shift, along_y[0], 0.0)
        along_y[3] = jnp.where(cell < shift, along_y[3], 0.0)
        along_y = [
            jnp.concatenate(along_y[:2], axis=0).astype(jnp.bfloat16),
            jnp.concatenate(along_y[2:], axis=0).astype(jnp.bfloat16),
        ]
        for x in range(XS):
            one = jnp.broadcast_to(along_x[x : x + 1, :], (16, particles)).astype(jnp.bfloat16)
            left[x * WINDOW : x * WINDOW + 16, :] = one * along_y[0]
            left[x * WINDOW + 16 : (x + 1) * WINDOW, :] = one * along_y[1]
        along_z = [gauss(8 * i, pz) for i in range(3)] + [jnp.zeros((8, particles), jnp.float32)]
        right[...] = jnp.concatenate(along_z, axis=0).astype(jnp.bfloat16)

    lane = lax.broadcasted_iota(jnp.int32, (1, LANES), 1)

    def settle(k, left, right):
        item = items[k]
        device, b = item // 16, item % 16
        y0 = device % count * own_rows + facts[device, 2 * bins + b]
        z0 = facts[device, 3 * bins + b]
        at = z0 & (block - 1)
        s0 = z0 // block * me & (count - 1)
        s1 = (z0 // block + 1) * me & (count - 1)
        rest = jnp.zeros((block - WINDOW, particles), jnp.bfloat16)
        value = lax.dot_general(
            left[...],
            jnp.concatenate([right[...], rest] * (LANES // block), axis=0),
            (((1,), (1,)), ((), ())),
            preferred_element_type=jnp.float32,
        )
        value = pltpu.roll(value, at, axis=1)
        base = y0 // 8 * 8
        for h in range(folds):
            spot = lane + h * LANES
            real = spot < block
            wrapped = (spot & (block - 1)) < at
            factor = jnp.where(
                real,
                jnp.where(wrapped, turn[s1], turn[s0]),
                jnp.where(wrapped, turn[count + s1], turn[count + s0]),
            )
            for x in range(XS):
                at_row = pl.multiple_of((h * XS + x) * pitch + base, 8)
                folded[pl.ds(at_row, WINDOW), :] += (
                    value[x * WINDOW : (x + 1) * WINDOW, :] * factor
                )

    for u in range(TOGETHER):
        build(u, lefts.at[u], rights.at[u])

    def group(g, carry):
        for half in range(2):
            here, there = half * TOGETHER, (1 - half) * TOGETHER
            k = (2 * g + half) * TOGETHER
            for u in range(TOGETHER):
                build(k + TOGETHER + u, lefts.at[there + u], rights.at[there + u])
                settle(k + u, lefts.at[here + u], rights.at[here + u])
        return carry

    lax.fori_loop(0, (total + 2 * TOGETHER - 1) // (2 * TOGETHER), group, 0)
    for h in range(folds):
        for x in range(XS):
            at_row = (h * XS + x) * pitch
            folded[at_row : at_row + WINDOW, :] += folded[at_row + NY : at_row + pitch, :]
    z_copy.wait()
    y_copy.wait()

    def transform(pair, t):
        lines = jnp.concatenate(
            [
                jnp.concatenate(
                    [
                        folded[
                            pl.ds((h * XS + pair * PAIR + x) * pitch + t, points, stride=SPLIT), :
                        ].astype(jnp.bfloat16)
                        for h in range(folds)
                    ],
                    axis=1,
                )
                for x in range(PAIR)
            ],
            axis=0,
        )
        along = lax.dot_general(
            ztab[...], lines, (((1,), (1,)), ((), ())), preferred_element_type=jnp.float32
        ).astype(jnp.bfloat16)
        along = jnp.concatenate(
            [
                jnp.concatenate(
                    [
                        along[:block, x * points : (x + 1) * points],
                        along[block:, x * points : (x + 1) * points],
                    ],
                    axis=1,
                )
                for x in range(PAIR)
            ],
            axis=0,
        )
        terms[pair % 2, t] = jnp.dot(along, ytab[t], preferred_element_type=jnp.float32)

    root = math.sqrt(0.5)

    def four(a, b, c, d):
        (ar, ai), (br, bi), (cr, ci), (dr, di) = a, b, c, d
        pr, pi, mr, mi = ar + cr, ai + ci, ar - cr, ai - ci
        qr, qi, nr, ni = br + dr, bi + di, br - dr, bi - di
        return (pr + qr, pi + qi), (mr + ni, mi - nr), (pr - qr, pi - qi), (mr - ni, mi + nr)

    def combine(pair, x, r):
        at_row = x * block + r
        term = [
            (
                terms[pair % 2, t, at_row : at_row + 8, :points],
                terms[pair % 2, t, at_row : at_row + 8, points:],
            )
            for t in range(SPLIT)
        ]
        even = four(term[0], term[2], term[4], term[6])
        odd = four(term[1], term[3], term[5], term[7])
        o1 = ((odd[1][0] + odd[1][1]) * root, (odd[1][1] - odd[1][0]) * root)
        o2 = (odd[2][1], -odd[2][0])
        o3 = ((odd[3][1] - odd[3][0]) * root, (odd[3][0] + odd[3][1]) * -root)
        slot = pair % 2 * PAIR + x
        for q, turned in enumerate((odd[0], o1, o2, o3)):
            for c in range(2):
                results[slot, c, r : r + 8, q * points : (q + 1) * points] = even[q][c] + turned[c]
                results[slot, c, r : r + 8, (q + 4) * points : (q + 5) * points] = (
                    even[q][c] - turned[c]
                )

    def leave(plane):
        return pltpu.make_async_copy(
            results.at[plane % (2 * PAIR)], out.at[:, plane], sent.at[plane % (2 * PAIR)]
        )

    pairs = XS // PAIR
    for t in range(SPLIT):
        transform(0, t)
    todo = [(x, r) for x in range(PAIR) for r in range(0, block, 8)]
    each = len(todo) // SPLIT
    for pair in range(pairs):
        for t in range(SPLIT):
            if pair + 1 < pairs:
                transform(pair + 1, t)
            for x, r in todo[t * each : (t + 1) * each]:
                plane = pair * PAIR + x
                if r == 0 and plane >= 2 * PAIR:
                    leave(plane - 2 * PAIR).wait()
                combine(pair, x, r)
                if r + 8 == block:
                    leave(plane).start()
    for plane in range(XS - 2 * PAIR, XS):
        leave(plane).wait()


def body(positions, forces, counts, anchors, helpers):
    bins, _, particles = positions.shape
    count = lax.axis_size("narrow")
    wide = lax.axis_size("wide")
    me = lax.axis_index("narrow")
    block = NZ // count
    own_rows = NY // count
    slabs = 1 + (PATCH + XS - 2) // XS
    slots = slabs * count
    stride = (2 * particles // LANES * bins + 1 + 7) // 8 * 8

    parts = pl.pallas_call(
        lambda *refs: gather_kernel(*refs, wide=wide, count=count, slabs=slabs, stride=stride),
        in_specs=[pl.BlockSpec(memory_space=pltpu.VMEM)] * 5,
        out_specs=pl.BlockSpec(memory_space=pl.ANY),
        out_shape=jax.ShapeDtypeStruct((slots, stride, LANES), jnp.int32),
        scratch_shapes=[
            pltpu.VMEM((stride, LANES), jnp.int32),
            pltpu.SemaphoreType.DMA((slots,)),
            pltpu.SemaphoreType.DMA((slots,)),
            pltpu.SemaphoreType.DMA,
        ],
        compiler_params=pltpu.CompilerParams(collective_id=0, has_side_effects=True),
        name="gather_particles",
    )(positions, forces, counts.reshape(1, bins), anchors, helpers.reshape(1, bins))
    ytab = jnp.asarray(y_tables())
    ztab = jnp.asarray(z_tables(block, count))
    turn = jnp.asarray(turns(count))
    meta = 2 * particles // LANES * bins

    spectrum, load = pl.pallas_call(
        lambda *refs: spectrum_kernel(
            *refs, bins=bins, block=block, count=count, own_rows=own_rows, slabs=slabs
        ),
        in_specs=[pl.BlockSpec(memory_space=pltpu.SMEM)]
        + [pl.BlockSpec(memory_space=pl.ANY)] * 3,
        out_specs=[pl.BlockSpec(memory_space=pl.ANY), pl.BlockSpec(memory_space=pltpu.VMEM)],
        scratch_shapes=[
            pltpu.VMEM((2 * block // LANES * XS * (NY + WINDOW), LANES), jnp.float32),
            pltpu.SMEM((slots, LANES), jnp.int32),
            pltpu.VMEM((slots, stride, LANES), jnp.int32),
            pltpu.VMEM((slots * meta, LANES), jnp.float32),
            pltpu.VMEM((slots * meta, LANES), jnp.float32),
            pltpu.SMEM((slots * bins + 4 * TOGETHER,), jnp.int32),
            pltpu.VMEM(ztab.shape[1:], jnp.bfloat16),
            pltpu.VMEM(ytab.shape, jnp.bfloat16),
            pltpu.VMEM((2, SPLIT, PAIR * block, 2 * NY // SPLIT), jnp.float32),
            pltpu.VMEM((2 * PAIR, 2, block, NY), jnp.float32),
            pltpu.VMEM((2 * TOGETHER, XS * WINDOW, particles), jnp.bfloat16),
            pltpu.VMEM((2 * TOGETHER, WINDOW, particles), jnp.bfloat16),
            pltpu.SemaphoreType.DMA((4,)),
            pltpu.SemaphoreType.DMA((2 * PAIR,)),
        ],
        out_shape=[
            jax.ShapeDtypeStruct((2, XS, block, NY), jnp.float32),
            jax.ShapeDtypeStruct((1, 1), jnp.float32),
        ],
        compiler_params=pltpu.CompilerParams(vmem_limit_bytes=60 * 1024 * 1024),
        name="spread_and_transform",
    )(turn, parts, ztab, ytab)
    return (spectrum, load)


def solution(mesh):
    return jax.shard_map(
        body,
        mesh=mesh,
        in_specs=(
            P(("wide", "narrow"), None, None),
            P(("wide", "narrow"), None),
            P(("wide", "narrow")),
            P(None, ("wide", "narrow")),
            P(("wide", "narrow"), None),
        ),
        out_specs=(P(None, "wide", "narrow", None), P("wide", "narrow")),
        check_vma=False,
    )
```

```python
import math

import jax
import jax.numpy as jnp
import numpy as np
from jax import lax
from jax.experimental import pallas as pl
from jax.experimental.pallas import tpu as pltpu
from jax.sharding import PartitionSpec as P

XS = 8
NY = 1024
NZ = 1024
PATCH = 24
SPLIT = 8
WINDOW = 32
TOGETHER = 4
LANES = 128
PAIR = 2

LOWEST, SPAN = 6.0, 12.0
POSITION_STEPS = 65535.0
FORCE_STEPS = 32000.0
FORCE_ZERO = 32768

spread_rate = 0.08
spread_root = math.sqrt(spread_rate / math.log(2.0))
two_pi = 2.0 * math.pi


def y_tables():
    points = NY // SPLIT
    y = np.arange(points)[None, :] * SPLIT + np.arange(SPLIT)[:, None]
    phase = (y[:, :, None] * np.arange(points)[None, None, :]) % NY
    angle = phase * (two_pi / NY)
    cos = np.cos(angle) / math.sqrt(NY)
    sin = np.sin(angle) / math.sqrt(NY)
    upper = np.concatenate([cos, -sin], axis=2)
    lower = np.concatenate([sin, cos], axis=2)
    return np.concatenate([upper, lower], axis=1).astype(np.float32).astype(jnp.bfloat16)


def z_tables(block, count):
    frequency = np.arange(block)[None, :] * count + np.arange(count)[:, None]
    phase = frequency[:, :, None] * np.arange(block)[None, None, :] % NZ
    angle = phase * (two_pi / NZ)
    cos = np.cos(angle) / math.sqrt(NZ)
    sin = np.sin(angle) / math.sqrt(NZ)
    top = np.concatenate([cos, sin], axis=2)
    bottom = np.concatenate([-sin, cos], axis=2)
    return np.concatenate([top, bottom], axis=1).astype(np.float32).astype(jnp.bfloat16)


def turns(count):
    angle = np.arange(count) * (two_pi / count)
    return np.concatenate([np.cos(angle), -np.sin(angle)]).astype(np.float32)


def encode(positions, forces, counts, anchors, helpers, own, bins):
    particles = forces.shape[1]
    scale = POSITION_STEPS / SPAN

    def place(c):
        code = (positions[:, c, :] - LOWEST) * scale + 0.5
        return jnp.clip(code, 0.0, POSITION_STEPS).astype(jnp.int32)

    lane = lax.broadcasted_iota(jnp.int32, (bins, LANES), 1)
    bin_of = lax.broadcasted_iota(jnp.int32, (bins, LANES), 0)
    row = jnp.concatenate(
        [
            counts[...],
            anchors[0:1, :],
            anchors[1:2, :],
            anchors[2:3, :],
            helpers[...],
            jnp.zeros((1, LANES - 5 * bins), jnp.int32),
        ],
        axis=1,
    )
    spread_counts = jnp.broadcast_to(row.astype(jnp.float32), (bins, LANES))
    live = jnp.sum(jnp.where(lane == bin_of, spread_counts, 0.0), axis=1, keepdims=True)
    slot = lax.broadcasted_iota(jnp.int32, (bins, particles), 1).astype(jnp.float32)
    force = jnp.where(slot < live, forces[...], 0.0)
    largest = jnp.max(jnp.max(jnp.abs(force), axis=1, keepdims=True), axis=0, keepdims=True)
    power = jnp.ceil(jnp.log2(jnp.maximum(largest, 1e-36)))
    code = (force * jnp.exp2(-power) * FORCE_STEPS + (FORCE_ZERO + 0.5)).astype(jnp.int32)
    first = lax.shift_left(place(0), 16) | place(1)
    second = lax.shift_left(place(2), 16) | code
    for h in range(particles // LANES):
        own[h * bins : (h + 1) * bins, :] = first[:, h * LANES : (h + 1) * LANES]
    for h in range(particles // LANES):
        at = particles // LANES * bins + h * bins
        own[at : at + bins, :] = second[:, h * LANES : (h + 1) * LANES]
    at = 2 * particles // LANES * bins
    lane = lax.broadcasted_iota(jnp.int32, (1, LANES), 1)
    power = jnp.broadcast_to(power.astype(jnp.int32), (1, LANES))
    alive = jnp.where((lane < bins) & (row > 0), 1.0, 0.0)
    alive = jnp.sum(alive, axis=1, keepdims=True).astype(jnp.int32)
    row = jnp.where(lane == 5 * bins, power, row)
    own[at : at + 1, :] = jnp.where(lane == 5 * bins + 1, alive, row)


def gather_kernel(
    positions, forces, counts, anchors, helpers, parts, folded, block_own, send, receive, local,
    *, wide, count, slabs, stride
):
    w, n = lax.axis_index("wide"), lax.axis_index("narrow")
    chips = count // 2
    z, core = n // 2, n % 2
    other = z * 2 + (1 - core)

    used = 2 * forces.shape[1] // LANES * forces.shape[0] + 1

    def place(distance, index):
        return parts.at[distance * count + index, pl.ds(0, used)]

    def at(distance, index):
        return receive.at[distance * count + index]

    def later(distance):
        return (w + distance) % wide

    def across(step):
        chip, bit = z, 1
        while bit <= step:
            if step & bit:
                chip = chip + bit - 2 * bit * (z // bit % 2)
            bit *= 2
        return chip * 2 + core

    peers = [across(step) for step in range(1, chips)]
    barrier = pltpu.get_barrier_semaphore()
    for peer in peers + [other]:
        pl.semaphore_signal(
            barrier, inc=1, device_id=(w, peer), device_id_type=pl.DeviceIdType.MESH
        )
    for distance in range(1, slabs):
        pl.semaphore_signal(
            barrier,
            inc=1,
            device_id=((w + wide - distance) % wide, n),
            device_id_type=pl.DeviceIdType.MESH,
        )
    own = block_own.at[pl.ds(0, used), :]
    encode(positions, forces, counts, anchors, helpers, block_own, forces.shape[0])
    pl.semaphore_wait(barrier, chips + slabs - 1)

    sent = []

    def push(source, target, distance, index):
        copy = pltpu.make_async_remote_copy(
            src_ref=source,
            dst_ref=place(distance, index),
            send_sem=send.at[len(sent)],
            recv_sem=at(distance, index),
            device_id=target,
            device_id_type=pl.DeviceIdType.MESH,
        )
        copy.start()
        sent.append(copy)

    def arrived(distance, index):
        pltpu.make_async_remote_copy(
            src_ref=own,
            dst_ref=place(distance, index),
            send_sem=send.at[0],
            recv_sem=at(distance, index),
            device_id=(w, other),
            device_id_type=pl.DeviceIdType.MESH,
        ).wait_recv()

    for peer in peers:
        push(own, (w, peer), 0, n)
    for distance in range(1, slabs):
        push(own, (later(distance), n), distance, n)
    push(own, (w, other), 0, n)
    keep = pltpu.make_async_copy(own, place(0, n), local)
    keep.start()
    sources = [n] + peers
    zero_rows = folded.shape[0] // (slabs * count)

    def clear(i, carry):
        at_row = pl.multiple_of(i * zero_rows, 8)
        folded[pl.ds(at_row, zero_rows), :] = jnp.zeros((zero_rows, LANES), jnp.float32)
        return carry

    lax.fori_loop(0, slabs * count, clear, 0)
    for source in sources[1:]:
        arrived(0, source)
        for distance in range(1, slabs):
            push(place(0, source), (later(distance), n), distance, source)
        push(place(0, source), (w, other), 0, source)
    for source in sources:
        for distance in range(1, slabs):
            arrived(distance, source)
            push(place(distance, source), (w, other), distance, source)
    for distance in range(slabs):
        for chip in range(chips):
            arrived(distance, chip * 2 + (1 - core))
    for copy in sent:
        copy.wait_send()
    keep.wait()


def spectrum_kernel(
    turn, coded, _, ztab_hbm, ytab_hbm, out, load, folded, facts, upper, lower, items,
    ztab, ytab, terms, results, sems, sent, *work,
    bins, block, count, own_rows, slabs
):
    lefts, helds, acrosses = (work[i * 2 * TOGETHER : (i + 1) * 2 * TOGETHER] for i in range(3))
    me = lax.axis_index("narrow")
    slots = slabs * count
    halves = lefts[0].shape[1] // LANES
    count_bits = count.bit_length() - 1
    block_bits = block.bit_length() - 1
    particles = halves * LANES
    half_rows = halves * bins
    meta = 2 * half_rows
    folds = 2 * block // LANES
    step = SPLIT + 1
    pitch = ((NY + WINDOW) // SPLIT * step + slots - 1) // slots * slots
    points = NY // SPLIT

    to_smem = pltpu.make_async_copy(coded.at[:, meta, :], facts, sems.at[0])
    z_copy = pltpu.make_async_copy(ztab_hbm.at[me], ztab, sems.at[2])
    y_copy = pltpu.make_async_copy(ytab_hbm, ytab, sems.at[3])
    to_smem.start()
    z_copy.start()
    y_copy.start()
    to_smem.wait()

    home = jnp.concatenate([coded[d, meta : meta + 1, :] for d in range(count)], axis=0)
    helper = pltpu.roll(home, LANES - 4 * bins, axis=1)
    lane = lax.broadcasted_iota(jnp.int32, home.shape, 1)
    mine = jnp.where((lane < bins) & (helper == me), home, 0).astype(jnp.float32)
    load[...] = jnp.sum(mine, keepdims=True).reshape(1, 1) / particles

    def per_device(device, total):
        alive = facts[device, 5 * bins + 1]
        power = facts[device, 5 * bins].astype(jnp.float32)
        for b in range(bins):
            items[total + b] = device * 16 + b
        gain = jnp.exp2(jnp.full((1, LANES), power)) * (1.0 / FORCE_STEPS)
        word = coded[device, :meta, :]
        high = lax.shift_right_logical(word, 16).astype(jnp.float32)
        low = (word & 65535).astype(jnp.float32)
        unit = SPAN / POSITION_STEPS * spread_root
        upper[pl.ds(pl.multiple_of(device * meta, 8), meta), :] = high * unit + LOWEST * spread_root
        lower[pl.ds(pl.multiple_of(device * meta, 8), half_rows), :] = (
            low[:half_rows] * unit + LOWEST * spread_root
        )
        lower[pl.ds(pl.multiple_of(device * meta + half_rows, 8), half_rows), :] = (
            low[half_rows:] - FORCE_ZERO
        ) * gain
        return total + alive

    total = lax.fori_loop(0, slots, per_device, 0)
    for extra in range(4 * TOGETHER):
        items[total + extra] = 0

    cell = lax.broadcasted_iota(jnp.int32, (8, particles), 0)
    steps8 = cell.astype(jnp.float32) * spread_root

    def gauss(first, place):
        away = (steps8 + first * spread_root) - place
        return jnp.exp2(-(away * away))

    def line(ref, row):
        return jnp.concatenate([ref[pl.ds(row + h * bins, 1), :] for h in range(halves)], axis=1)

    def build(k, left, held, across):
        item = items[k]
        device, b = item >> 4, item & 15
        r = device * meta + b
        x0 = (device >> count_bits) * XS - facts[device, bins + b]
        shift = facts[device, 3 * bins + b] & 7
        at = pl.multiple_of(facts[device, 3 * bins + b] & (block - 8), 8)
        px = line(upper, r) - x0.astype(jnp.float32) * spread_root
        py = line(lower, r)
        pz = line(upper, r + half_rows) + shift.astype(jnp.float32) * spread_root
        force = line(lower, r + half_rows)
        force = jnp.where(k < total, force, jnp.zeros_like(force))
        along_x = gauss(0, px) * force
        along_x = jnp.where((cell >= -x0) & (cell < PATCH - x0), along_x, 0.0)
        along_x = jnp.concatenate([along_x, along_x], axis=0).astype(jnp.bfloat16)
        for i in range(PATCH // 8):
            across[8 * i : 8 * i + 8, :] = gauss(8 * i, py)
        for j in range(0, PATCH, 2):
            one = [jnp.broadcast_to(across[j + i : j + i + 1, :], (8, particles)) for i in range(2)]
            one = jnp.concatenate(one, axis=0).astype(jnp.bfloat16)
            left[XS * j : XS * (j + 2), :] = along_x * one
        along_z = [gauss(8 * i, pz) for i in range(4)]
        along_z[0] = jnp.where(cell >= shift, along_z[0], 0.0)
        along_z[3] = jnp.where(cell < shift, along_z[3], 0.0)
        held[pl.ds(at, WINDOW), :] = jnp.concatenate(along_z, axis=0)

    lane = lax.broadcasted_iota(jnp.int32, (1, LANES), 1)

    def settle(k, left, held):
        item = items[k]
        device, b = item >> 4, item & 15
        y0 = (device & (count - 1)) * own_rows + facts[device, 2 * bins + b]
        z0 = facts[device, 3 * bins + b]
        at = pl.multiple_of(z0 & (block - 8), 8)
        turned = (z0 >> block_bits) * me
        s0 = turned & (count - 1)
        s1 = (turned + me) & (count - 1)
        right = jnp.concatenate(
            [held[:WINDOW, :] + held[block:, :], held[WINDOW:block, :]], axis=0
        ).astype(jnp.bfloat16)
        held[pl.ds(at, WINDOW), :] = jnp.zeros((WINDOW, particles), jnp.float32)
        value = lax.dot_general(
            left[...],
            jnp.concatenate([right] * (LANES // block), axis=0),
            (((1,), (1,)), ((), ())),
            preferred_element_type=jnp.float32,
        )
        factors = []
        for h in range(folds):
            spot = lane + h * LANES
            wrapped = (spot & (block - 1)) < at
            factor = jnp.where(
                spot < block,
                jnp.where(wrapped, turn[s1], turn[s0]),
                jnp.where(wrapped, turn[count + s1], turn[count + s0]),
            )
            factors.append(factor)
        base = y0 + (y0 >> 3)
        spots = []
        for i in range(PATCH // SPLIT):
            for j in range(SPLIT):
                first = base + jnp.where((y0 & 7) + j >= SPLIT, j + 1, j)
                spots.append([pl.multiple_of((first + (h * pitch + i * step)) * XS, 8) for h in range(folds)])
        olds = [[folded[pl.ds(spot[h], XS), :] for h in range(folds)] for spot in spots]
        for j, spot in enumerate(spots):
            for h in range(folds):
                one = value[j * XS : (j + 1) * XS, :]
                folded[pl.ds(spot[h], XS), :] = olds[j][h] + one * factors[h]

    for held in helds:
        held[...] = jnp.zeros_like(held)
    for u in range(TOGETHER):
        build(u, lefts[u], helds[u], acrosses[u])

    def group(g, carry):
        for half in range(2):
            here, there = half * TOGETHER, (1 - half) * TOGETHER
            k = (2 * g + half) * TOGETHER
            for u in range(TOGETHER):
                build(
                    k + TOGETHER + u, lefts[there + u], helds[there + u], acrosses[there + u]
                )
                settle(k + u, lefts[here + u], helds[here + u])
        return carry

    lax.fori_loop(0, (total + 2 * TOGETHER - 1) // (2 * TOGETHER), group, 0)
    for h in range(folds):
        at_row = h * pitch * XS
        over = at_row + NY // SPLIT * step * XS
        rows = PATCH // SPLIT * step * XS
        folded[at_row : at_row + rows, :] += folded[over : over + rows, :]
    z_copy.wait()
    y_copy.wait()

    def transform(pair, t):
        lines = jnp.concatenate(
            [
                jnp.concatenate(
                    [
                        folded[
                            pl.ds((h * pitch + t) * XS + pair * PAIR + x, points, stride=step * XS), :
                        ].astype(jnp.bfloat16)
                        for h in range(folds)
                    ],
                    axis=1,
                )
                for x in range(PAIR)
            ],
            axis=0,
        )
        along = lax.dot_general(
            ztab[...], lines, (((1,), (1,)), ((), ())), preferred_element_type=jnp.float32
        ).astype(jnp.bfloat16)
        along = jnp.concatenate(
            [
                jnp.concatenate(
                    [
                        along[:block, x * points : (x + 1) * points],
                        along[block:, x * points : (x + 1) * points],
                    ],
                    axis=1,
                )
                for x in range(PAIR)
            ],
            axis=0,
        )
        terms[pair % 2, t] = jnp.dot(along, ytab[t], preferred_element_type=jnp.float32)

    root = math.sqrt(0.5)

    def four(a, b, c, d):
        (ar, ai), (br, bi), (cr, ci), (dr, di) = a, b, c, d
        pr, pi, mr, mi = ar + cr, ai + ci, ar - cr, ai - ci
        qr, qi, nr, ni = br + dr, bi + di, br - dr, bi - di
        return (pr + qr, pi + qi), (mr + ni, mi - nr), (pr - qr, pi - qi), (mr - ni, mi + nr)

    def combine(pair, x, r):
        at_row = x * block + r
        term = [
            (
                terms[pair % 2, t, at_row : at_row + 8, :points],
                terms[pair % 2, t, at_row : at_row + 8, points:],
            )
            for t in range(SPLIT)
        ]
        even = four(term[0], term[2], term[4], term[6])
        odd = four(term[1], term[3], term[5], term[7])
        o1 = ((odd[1][0] + odd[1][1]) * root, (odd[1][1] - odd[1][0]) * root)
        o2 = (odd[2][1], -odd[2][0])
        o3 = ((odd[3][1] - odd[3][0]) * root, (odd[3][0] + odd[3][1]) * -root)
        slot = pair % 2 * PAIR + x
        for q, turned in enumerate((odd[0], o1, o2, o3)):
            for c in range(2):
                results[slot, c, r : r + 8, q * points : (q + 1) * points] = even[q][c] + turned[c]
                results[slot, c, r : r + 8, (q + 4) * points : (q + 5) * points] = (
                    even[q][c] - turned[c]
                )

    def leave(plane):
        return pltpu.make_async_copy(
            results.at[plane % (2 * PAIR)], out.at[:, plane], sent.at[plane % (2 * PAIR)]
        )

    pairs = XS // PAIR
    for t in range(SPLIT):
        transform(0, t)
    todo = [(x, r) for x in range(PAIR) for r in range(0, block, 8)]
    each = len(todo) // SPLIT
    for pair in range(pairs):
        for t in range(SPLIT):
            if pair + 1 < pairs:
                transform(pair + 1, t)
            for x, r in todo[t * each : (t + 1) * each]:
                plane = pair * PAIR + x
                if r == 0 and plane >= 2 * PAIR:
                    leave(plane - 2 * PAIR).wait()
                combine(pair, x, r)
                if r + 8 == block:
                    leave(plane).start()
    for plane in range(XS - 2 * PAIR, XS):
        leave(plane).wait()


def in_hbm(x):
    return pltpu.with_memory_space_constraint(x, pltpu.HBM)


def body(positions, forces, counts, anchors, helpers):
    bins, _, particles = positions.shape
    count = lax.axis_size("narrow")
    wide = lax.axis_size("wide")
    me = lax.axis_index("narrow")
    block = NZ // count
    own_rows = NY // count
    slabs = 1 + (PATCH + XS - 2) // XS
    slots = slabs * count
    stride = (2 * particles // LANES * bins + 1 + 7) // 8 * 8

    pitch = ((NY + WINDOW) // SPLIT * (SPLIT + 1) + slots - 1) // slots * slots
    folded_rows = 2 * block // LANES * pitch * XS
    parts, folded = pl.pallas_call(
        lambda *refs: gather_kernel(*refs, wide=wide, count=count, slabs=slabs, stride=stride),
        in_specs=[pl.BlockSpec(memory_space=pltpu.VMEM)] * 5,
        out_specs=[pl.BlockSpec(memory_space=pl.ANY), pl.BlockSpec(memory_space=pltpu.VMEM)],
        out_shape=[
            pltpu.VMEM((slots, stride, LANES), jnp.int32),
            pltpu.VMEM((folded_rows, LANES), jnp.float32),
        ],
        scratch_shapes=[
            pltpu.VMEM((stride, LANES), jnp.int32),
            pltpu.SemaphoreType.DMA((slots,)),
            pltpu.SemaphoreType.DMA((slots,)),
            pltpu.SemaphoreType.DMA,
        ],
        compiler_params=pltpu.CompilerParams(
            collective_id=0, has_side_effects=True, vmem_limit_bytes=16 * 1024 * 1024
        ),
        name="gather_particles",
    )(*map(in_hbm, (positions, forces, counts.reshape(1, bins), anchors, helpers.reshape(1, bins))))
    ytab = jnp.asarray(y_tables())
    ztab = jnp.asarray(z_tables(block, count))
    turn = jnp.asarray(turns(count))
    meta = 2 * particles // LANES * bins

    spectrum, load, _ = pl.pallas_call(
        lambda *refs: spectrum_kernel(
            *refs, bins=bins, block=block, count=count, own_rows=own_rows, slabs=slabs
        ),
        in_specs=[pl.BlockSpec(memory_space=pltpu.SMEM)]
        + [pl.BlockSpec(memory_space=pltpu.VMEM)] * 2
        + [pl.BlockSpec(memory_space=pl.ANY)] * 2,
        out_specs=[
            pl.BlockSpec(memory_space=pl.ANY),
            pl.BlockSpec(memory_space=pltpu.VMEM),
            pl.BlockSpec(memory_space=pltpu.VMEM),
        ],
        scratch_shapes=[
            pltpu.SMEM((slots, LANES), jnp.int32),
            pltpu.VMEM((slots * meta, LANES), jnp.float32),
            pltpu.VMEM((slots * meta, LANES), jnp.float32),
            pltpu.SMEM((slots * bins + 4 * TOGETHER,), jnp.int32),
            pltpu.VMEM(ztab.shape[1:], jnp.bfloat16),
            pltpu.VMEM(ytab.shape, jnp.bfloat16),
            pltpu.VMEM((2, SPLIT, PAIR * block, 2 * NY // SPLIT), jnp.float32),
            pltpu.VMEM((2 * PAIR, 2, block, NY), jnp.float32),
            pltpu.SemaphoreType.DMA((4,)),
            pltpu.SemaphoreType.DMA((2 * PAIR,)),
        ]
        + [pltpu.VMEM((XS * PATCH, particles), jnp.bfloat16)] * (2 * TOGETHER)
        + [pltpu.VMEM((block + WINDOW, particles), jnp.float32)] * (2 * TOGETHER)
        + [pltpu.VMEM((PATCH, particles), jnp.float32)] * (2 * TOGETHER),
        out_shape=[
            jax.ShapeDtypeStruct((2, XS, block, NY), jnp.float32),
            jax.ShapeDtypeStruct((1, 1), jnp.float32),
            pltpu.VMEM((folded_rows, LANES), jnp.float32),
        ],
        input_output_aliases={2: 2},
        compiler_params=pltpu.CompilerParams(vmem_limit_bytes=36 * 1024 * 1024),
        name="spread_and_transform",
    )(
        in_hbm(turn),
        pltpu.with_memory_space_constraint(parts, pltpu.VMEM),
        pltpu.with_memory_space_constraint(folded, pltpu.VMEM),
        in_hbm(ztab),
        in_hbm(ytab),
    )
    return (spectrum, load)


def solution(mesh):
    return jax.shard_map(
        body,
        mesh=mesh,
        in_specs=(
            P(("wide", "narrow"), None, None),
            P(("wide", "narrow"), None),
            P(("wide", "narrow")),
            P(None, ("wide", "narrow")),
            P(("wide", "narrow"), None),
        ),
        out_specs=(P(None, "wide", "narrow", None), P("wide", "narrow")),
        check_vma=False,
    )
```

```python
import math

import jax
import jax.numpy as jnp
import numpy as np
from jax import lax
from jax.experimental import pallas as pl
from jax.experimental.pallas import tpu as pltpu
from jax.sharding import PartitionSpec as P

XS = 8
NY = 1024
NZ = 1024
PATCH = 24
SPLIT = 8
WINDOW = 32
TOGETHER = 4
LANES = 128
PAIR = 2

LOWEST, SPAN = 6.0, 12.0
POSITION_STEPS = 65535.0
FORCE_STEPS = 32000.0
FORCE_ZERO = 32768

spread_rate = 0.08
spread_root = math.sqrt(spread_rate / math.log(2.0))
two_pi = 2.0 * math.pi


def y_tables():
    points = NY // SPLIT
    y = np.arange(points)[None, :] * SPLIT + np.arange(SPLIT)[:, None]
    phase = (y[:, :, None] * np.arange(points)[None, None, :]) % NY
    angle = phase * (two_pi / NY)
    cos = np.cos(angle) / math.sqrt(NY)
    sin = np.sin(angle) / math.sqrt(NY)
    upper = np.concatenate([cos, -sin], axis=2)
    lower = np.concatenate([sin, cos], axis=2)
    return np.concatenate([upper, lower], axis=1).astype(np.float32).astype(jnp.bfloat16)


def z_tables(block, count):
    frequency = np.arange(block)[None, :] * count + np.arange(count)[:, None]
    phase = frequency[:, :, None] * np.arange(block)[None, None, :] % NZ
    angle = phase * (two_pi / NZ)
    cos = np.cos(angle) / math.sqrt(NZ)
    sin = np.sin(angle) / math.sqrt(NZ)
    top = np.concatenate([cos, sin], axis=2)
    bottom = np.concatenate([-sin, cos], axis=2)
    return np.concatenate([top, bottom], axis=1).astype(np.float32).astype(jnp.bfloat16)


def turns(count):
    angle = np.arange(count) * (two_pi / count)
    return np.concatenate([np.cos(angle), -np.sin(angle)]).astype(np.float32)


def encode(positions, forces, counts, anchors, helpers, own, bins):
    particles = forces.shape[1]
    scale = POSITION_STEPS / SPAN

    def place(c):
        code = (positions[:, c, :] - LOWEST) * scale + 0.5
        return jnp.clip(code, 0.0, POSITION_STEPS).astype(jnp.int32)

    lane = lax.broadcasted_iota(jnp.int32, (bins, LANES), 1)
    bin_of = lax.broadcasted_iota(jnp.int32, (bins, LANES), 0)
    row = jnp.concatenate(
        [
            counts[...],
            anchors[0:1, :],
            anchors[1:2, :],
            anchors[2:3, :],
            helpers[...],
            jnp.zeros((1, LANES - 5 * bins), jnp.int32),
        ],
        axis=1,
    )
    spread_counts = jnp.broadcast_to(row.astype(jnp.float32), (bins, LANES))
    live = jnp.sum(jnp.where(lane == bin_of, spread_counts, 0.0), axis=1, keepdims=True)
    slot = lax.broadcasted_iota(jnp.int32, (bins, particles), 1).astype(jnp.float32)
    force = jnp.where(slot < live, forces[...], 0.0)
    largest = jnp.max(jnp.max(jnp.abs(force), axis=1, keepdims=True), axis=0, keepdims=True)
    power = jnp.ceil(jnp.log2(jnp.maximum(largest, 1e-36)))
    code = (force * jnp.exp2(-power) * FORCE_STEPS + (FORCE_ZERO + 0.5)).astype(jnp.int32)
    first = lax.shift_left(place(0), 16) | place(1)
    second = lax.shift_left(place(2), 16) | code
    for h in range(particles // LANES):
        own[h * bins : (h + 1) * bins, :] = first[:, h * LANES : (h + 1) * LANES]
    for h in range(particles // LANES):
        at = particles // LANES * bins + h * bins
        own[at : at + bins, :] = second[:, h * LANES : (h + 1) * LANES]
    at = 2 * particles // LANES * bins
    lane = lax.broadcasted_iota(jnp.int32, (1, LANES), 1)
    power = jnp.broadcast_to(power.astype(jnp.int32), (1, LANES))
    alive = jnp.where((lane < bins) & (row > 0), 1.0, 0.0)
    alive = jnp.sum(alive, axis=1, keepdims=True).astype(jnp.int32)
    row = jnp.where(lane == 5 * bins, power, row)
    own[at : at + 1, :] = jnp.where(lane == 5 * bins + 1, alive, row)


def gather_kernel(
    *refs, wide, count, slabs, stride
):
    given, refs = refs[:5], refs[5:]
    parts, folded, positions, forces, counts, anchors, helpers = refs[:7]
    block_own, send, receive, local, fetched = refs[7:]
    fetches = [
        pltpu.make_async_copy(source, target, fetched.at[i])
        for i, (source, target) in enumerate(zip(given, refs[2:7]))
    ]
    for fetch in fetches:
        fetch.start()
    w, n = lax.axis_index("wide"), lax.axis_index("narrow")
    chips = count // 2
    z, core = n // 2, n % 2
    other = z * 2 + (1 - core)

    used = 2 * forces.shape[1] // LANES * forces.shape[0] + 1

    def place(distance, index):
        return parts.at[distance * count + index, pl.ds(0, used)]

    def at(distance, index):
        return receive.at[distance * count + index]

    def later(distance):
        return (w + distance) % wide

    def across(step):
        chip, bit = z, 1
        while bit <= step:
            if step & bit:
                chip = chip + bit - 2 * bit * (z // bit % 2)
            bit *= 2
        return chip * 2 + core

    peers = [across(step) for step in range(1, chips)]
    barrier = pltpu.get_barrier_semaphore()
    for peer in peers + [other]:
        pl.semaphore_signal(
            barrier, inc=1, device_id=(w, peer), device_id_type=pl.DeviceIdType.MESH
        )
    for distance in range(1, slabs):
        pl.semaphore_signal(
            barrier,
            inc=1,
            device_id=((w + wide - distance) % wide, n),
            device_id_type=pl.DeviceIdType.MESH,
        )
    own = block_own.at[pl.ds(0, used), :]
    for fetch in fetches:
        fetch.wait()
    encode(positions, forces, counts, anchors, helpers, block_own, forces.shape[0])
    pl.semaphore_wait(barrier, chips + slabs - 1)

    sent = []

    def push(source, target, distance, index):
        copy = pltpu.make_async_remote_copy(
            src_ref=source,
            dst_ref=place(distance, index),
            send_sem=send.at[len(sent)],
            recv_sem=at(distance, index),
            device_id=target,
            device_id_type=pl.DeviceIdType.MESH,
        )
        copy.start()
        sent.append(copy)

    def arrived(distance, index):
        pltpu.make_async_remote_copy(
            src_ref=own,
            dst_ref=place(distance, index),
            send_sem=send.at[0],
            recv_sem=at(distance, index),
            device_id=(w, other),
            device_id_type=pl.DeviceIdType.MESH,
        ).wait_recv()

    for peer in peers:
        push(own, (w, peer), 0, n)
    for distance in range(1, slabs):
        push(own, (later(distance), n), distance, n)
    push(own, (w, other), 0, n)
    keep = pltpu.make_async_copy(own, place(0, n), local)
    keep.start()
    sources = [n] + peers
    zero_rows = folded.shape[0] // (slabs * count)

    def clear(i, carry):
        at_row = pl.multiple_of(i * zero_rows, 8)
        folded[pl.ds(at_row, zero_rows), :] = jnp.zeros((zero_rows, LANES), jnp.float32)
        return carry

    lax.fori_loop(0, slabs * count, clear, 0)
    for source in sources[1:]:
        arrived(0, source)
        for distance in range(1, slabs):
            push(place(0, source), (later(distance), n), distance, source)
        push(place(0, source), (w, other), 0, source)
    for source in sources:
        for distance in range(1, slabs):
            arrived(distance, source)
            push(place(distance, source), (w, other), distance, source)
    for distance in range(slabs):
        for chip in range(chips):
            arrived(distance, chip * 2 + (1 - core))
    for copy in sent:
        copy.wait_send()
    keep.wait()


def spectrum_kernel(
    coded, _, ztab_hbm, ytab_hbm, out, load, folded, turn, facts, upper, lower, items,
    ztab, ytab, results, sems, sent, *work,
    bins, block, count, own_rows, slabs
):
    lefts, helds, acrosses = (work[i * 2 * TOGETHER : (i + 1) * 2 * TOGETHER] for i in range(3))
    me = lax.axis_index("narrow")
    slots = slabs * count
    halves = lefts[0].shape[1] // LANES
    count_bits = count.bit_length() - 1
    block_bits = block.bit_length() - 1
    particles = halves * LANES
    half_rows = halves * bins
    meta = 2 * half_rows
    folds = 2 * block // LANES
    step = SPLIT + 1
    pitch = ((NY + WINDOW) // SPLIT * step + slots - 1) // slots * slots
    points = NY // SPLIT

    to_smem = pltpu.make_async_copy(coded.at[:, meta, :], facts, sems.at[0])
    z_copy = pltpu.make_async_copy(ztab_hbm.at[me], ztab, sems.at[2])
    y_copy = pltpu.make_async_copy(ytab_hbm, ytab, sems.at[3])
    to_smem.start()
    z_copy.start()
    y_copy.start()
    for i, part in enumerate(turns(count)):
        turn[i] = jnp.float32(float(part))

    home = jnp.concatenate([coded[d, meta : meta + 1, :] for d in range(count)], axis=0)
    helper = pltpu.roll(home, LANES - 4 * bins, axis=1)
    lane = lax.broadcasted_iota(jnp.int32, home.shape, 1)
    mine = jnp.where((lane < bins) & (helper == me), home, 0).astype(jnp.float32)
    load[...] = jnp.sum(mine, keepdims=True).reshape(1, 1) / particles

    def decode(device):
        power = coded[device, meta : meta + 1, 5 * bins : 5 * bins + 1].astype(jnp.float32)
        gain = jnp.exp2(power) * (1.0 / FORCE_STEPS)
        word = coded[device, :meta, :]
        high = lax.shift_right_logical(word, 16).astype(jnp.float32)
        low = (word & 65535).astype(jnp.float32)
        unit = SPAN / POSITION_STEPS * spread_root
        at_row = pl.multiple_of(device * meta, 8)
        upper[pl.ds(at_row, meta), :] = high * unit + LOWEST * spread_root
        lower[pl.ds(at_row, half_rows), :] = low[:half_rows] * unit + LOWEST * spread_root
        lower[pl.ds(pl.multiple_of(at_row + half_rows, 8), half_rows), :] = (
            low[half_rows:] - FORCE_ZERO
        ) * gain

    def decode_some(i, carry):
        for k in range(4):
            decode(4 * i + k)
        return carry

    lax.fori_loop(0, slots // 4, decode_some, 0)
    to_smem.wait()

    def collect(i, total):
        for k in range(4):
            device = 4 * i + k
            for b in range(bins):
                items[total + b] = device * 16 + b
            total = total + facts[device, 5 * bins + 1]
        return total

    total = lax.fori_loop(0, slots // 4, collect, 0)
    for extra in range(4 * TOGETHER):
        items[total + extra] = 0

    cell = lax.broadcasted_iota(jnp.int32, (8, particles), 0)
    steps8 = cell.astype(jnp.float32) * spread_root

    def gauss(first, place):
        away = (steps8 + first * spread_root) - place
        return jnp.exp2(-(away * away))

    def line(ref, row):
        return jnp.concatenate([ref[pl.ds(row + h * bins, 1), :] for h in range(halves)], axis=1)

    def build(k, left, held, across):
        item = items[k]
        device, b = item >> 4, item & 15
        r = device * meta + b
        x0 = (device >> count_bits) * XS - facts[device, bins + b]
        shift = facts[device, 3 * bins + b] & 7
        at = pl.multiple_of(facts[device, 3 * bins + b] & (block - 8), 8)
        px = line(upper, r) - x0.astype(jnp.float32) * spread_root
        py = line(lower, r)
        pz = line(upper, r + half_rows) + shift.astype(jnp.float32) * spread_root
        force = line(lower, r + half_rows)
        force = jnp.where(k < total, force, jnp.zeros_like(force))
        along_x = gauss(0, px) * force
        along_x = jnp.where((cell >= -x0) & (cell < PATCH - x0), along_x, 0.0)
        along_x = jnp.concatenate([along_x, along_x], axis=0).astype(jnp.bfloat16)
        for i in range(PATCH // 8):
            across[8 * i : 8 * i + 8, :] = gauss(8 * i, py)
        for j in range(0, PATCH, 2):
            one = [jnp.broadcast_to(across[j + i : j + i + 1, :], (8, particles)) for i in range(2)]
            one = jnp.concatenate(one, axis=0).astype(jnp.bfloat16)
            left[XS * j : XS * (j + 2), :] = along_x * one
        along_z = [gauss(8 * i, pz) for i in range(4)]
        along_z[0] = jnp.where(cell >= shift, along_z[0], 0.0)
        along_z[3] = jnp.where(cell < shift, along_z[3], 0.0)
        held[pl.ds(at, WINDOW), :] = jnp.concatenate(along_z, axis=0)

    lane = lax.broadcasted_iota(jnp.int32, (1, LANES), 1)

    def settle(k, left, held):
        item = items[k]
        device, b = item >> 4, item & 15
        y0 = (device & (count - 1)) * own_rows + facts[device, 2 * bins + b]
        z0 = facts[device, 3 * bins + b]
        at = pl.multiple_of(z0 & (block - 8), 8)
        turned = (z0 >> block_bits) * me
        s0 = turned & (count - 1)
        s1 = (turned + me) & (count - 1)
        right = jnp.concatenate(
            [held[:WINDOW, :] + held[block:, :], held[WINDOW:block, :]], axis=0
        ).astype(jnp.bfloat16)
        held[pl.ds(at, WINDOW), :] = jnp.zeros((WINDOW, particles), jnp.float32)
        value = lax.dot_general(
            left[...],
            jnp.concatenate([right] * (LANES // block), axis=0),
            (((1,), (1,)), ((), ())),
            preferred_element_type=jnp.float32,
        )
        factors = []
        for h in range(folds):
            spot = lane + h * LANES
            wrapped = (spot & (block - 1)) < at
            factor = jnp.where(
                spot < block,
                jnp.where(wrapped, turn[s1], turn[s0]),
                jnp.where(wrapped, turn[count + s1], turn[count + s0]),
            )
            factors.append(factor)
        base = y0 + (y0 >> 3)
        spots = []
        for i in range(PATCH // SPLIT):
            for j in range(SPLIT):
                first = base + jnp.where((y0 & 7) + j >= SPLIT, j + 1, j)
                spots.append([pl.multiple_of((first + (h * pitch + i * step)) * XS, 8) for h in range(folds)])
        olds = [[folded[pl.ds(spot[h], XS), :] for h in range(folds)] for spot in spots]
        for j, spot in enumerate(spots):
            for h in range(folds):
                one = value[j * XS : (j + 1) * XS, :]
                folded[pl.ds(spot[h], XS), :] = olds[j][h] + one * factors[h]

    for held in helds:
        held[...] = jnp.zeros_like(held)
    for u in range(TOGETHER):
        build(u, lefts[u], helds[u], acrosses[u])

    def group(g, carry):
        for half in range(2):
            here, there = half * TOGETHER, (1 - half) * TOGETHER
            k = (2 * g + half) * TOGETHER
            for u in range(TOGETHER):
                build(
                    k + TOGETHER + u, lefts[there + u], helds[there + u], acrosses[there + u]
                )
                settle(k + u, lefts[here + u], helds[here + u])
        return carry

    lax.fori_loop(0, (total + 2 * TOGETHER - 1) // (2 * TOGETHER), group, 0)
    for h in range(folds):
        at_row = h * pitch * XS
        over = at_row + NY // SPLIT * step * XS
        rows = PATCH // SPLIT * step * XS
        folded[at_row : at_row + rows, :] += folded[over : over + rows, :]
    z_copy.wait()
    y_copy.wait()

    terms = {}

    def transform(pair, t):
        lines = jnp.concatenate(
            [
                jnp.concatenate(
                    [
                        folded[
                            pl.ds((h * pitch + t) * XS + pair * PAIR + x, points, stride=step * XS), :
                        ].astype(jnp.bfloat16)
                        for h in range(folds)
                    ],
                    axis=1,
                )
                for x in range(PAIR)
            ],
            axis=0,
        )
        along = lax.dot_general(
            ztab[...], lines, (((1,), (1,)), ((), ())), preferred_element_type=jnp.float32
        ).astype(jnp.bfloat16)
        along = jnp.concatenate(
            [
                jnp.concatenate(
                    [
                        along[:block, x * points : (x + 1) * points],
                        along[block:, x * points : (x + 1) * points],
                    ],
                    axis=1,
                )
                for x in range(PAIR)
            ],
            axis=0,
        )
        terms[pair % 2, t] = jnp.dot(along, ytab[t], preferred_element_type=jnp.float32)

    root = math.sqrt(0.5)

    def four(a, b, c, d):
        (ar, ai), (br, bi), (cr, ci), (dr, di) = a, b, c, d
        pr, pi, mr, mi = ar + cr, ai + ci, ar - cr, ai - ci
        qr, qi, nr, ni = br + dr, bi + di, br - dr, bi - di
        return (pr + qr, pi + qi), (mr + ni, mi - nr), (pr - qr, pi - qi), (mr - ni, mi + nr)

    def combine(pair, x, r):
        at_row = x * block + r
        term = [
            (
                terms[pair % 2, t][at_row : at_row + 8, :points],
                terms[pair % 2, t][at_row : at_row + 8, points:],
            )
            for t in range(SPLIT)
        ]
        even = four(term[0], term[2], term[4], term[6])
        odd = four(term[1], term[3], term[5], term[7])
        o1 = ((odd[1][0] + odd[1][1]) * root, (odd[1][1] - odd[1][0]) * root)
        o2 = (odd[2][1], -odd[2][0])
        o3 = ((odd[3][1] - odd[3][0]) * root, (odd[3][0] + odd[3][1]) * -root)
        slot = pair * PAIR + x
        for q, turned in enumerate((odd[0], o1, o2, o3)):
            for c in range(2):
                results[slot, c, r : r + 8, q * points : (q + 1) * points] = even[q][c] + turned[c]
                results[slot, c, r : r + 8, (q + 4) * points : (q + 5) * points] = (
                    even[q][c] - turned[c]
                )

    def leave(plane):
        return pltpu.make_async_copy(
            results.at[plane], out.at[:, plane], sent.at[plane]
        )

    pairs = XS // PAIR
    todo = [(x, r) for x in range(PAIR) for r in range(0, block, 8)]
    each = len(todo) // SPLIT
    for pair in range(pairs):
        for t in range(SPLIT):
            transform(pair, t)
        for t in range(SPLIT):
            for x, r in todo[t * each : (t + 1) * each]:
                plane = pair * PAIR + x
                combine(pair, x, r)
                if r + 8 == block:
                    leave(plane).start()
    for plane in range(XS):
        leave(plane).wait()


def in_hbm(x):
    return pltpu.with_memory_space_constraint(x, pltpu.HBM)


def body(positions, forces, counts, anchors, helpers):
    bins, _, particles = positions.shape
    count = lax.axis_size("narrow")
    wide = lax.axis_size("wide")
    me = lax.axis_index("narrow")
    block = NZ // count
    own_rows = NY // count
    slabs = 1 + (PATCH + XS - 2) // XS
    slots = slabs * count
    stride = (2 * particles // LANES * bins + 1 + 7) // 8 * 8

    pitch = ((NY + WINDOW) // SPLIT * (SPLIT + 1) + slots - 1) // slots * slots
    folded_rows = 2 * block // LANES * pitch * XS
    parts, folded = pl.pallas_call(
        lambda *refs: gather_kernel(*refs, wide=wide, count=count, slabs=slabs, stride=stride),
        in_specs=[pl.BlockSpec(memory_space=pl.ANY)] * 5,
        out_specs=[pl.BlockSpec(memory_space=pl.ANY), pl.BlockSpec(memory_space=pltpu.VMEM)],
        out_shape=[
            pltpu.VMEM((slots, stride, LANES), jnp.int32),
            pltpu.VMEM((folded_rows, LANES), jnp.float32),
        ],
        scratch_shapes=[
            pltpu.VMEM(positions.shape, jnp.float32),
            pltpu.VMEM(forces.shape, jnp.float32),
            pltpu.VMEM((1, bins), jnp.int32),
            pltpu.VMEM(anchors.shape, jnp.int32),
            pltpu.VMEM((1, bins), jnp.int32),
            pltpu.VMEM((stride, LANES), jnp.int32),
            pltpu.SemaphoreType.DMA((slots,)),
            pltpu.SemaphoreType.DMA((slots,)),
            pltpu.SemaphoreType.DMA,
            pltpu.SemaphoreType.DMA((5,)),
        ],
        compiler_params=pltpu.CompilerParams(
            collective_id=0, has_side_effects=True, vmem_limit_bytes=16 * 1024 * 1024
        ),
        name="gather_particles",
    )(*map(in_hbm, (positions, forces, counts.reshape(1, bins), anchors, helpers.reshape(1, bins))))
    ytab = jnp.asarray(y_tables())
    ztab = jnp.asarray(z_tables(block, count))
    meta = 2 * particles // LANES * bins

    spectrum, load, _ = pl.pallas_call(
        lambda *refs: spectrum_kernel(
            *refs, bins=bins, block=block, count=count, own_rows=own_rows, slabs=slabs
        ),
        in_specs=[pl.BlockSpec(memory_space=pltpu.VMEM)] * 2
        + [pl.BlockSpec(memory_space=pl.ANY)] * 2,
        out_specs=[
            pl.BlockSpec(memory_space=pl.ANY),
            pl.BlockSpec(memory_space=pltpu.VMEM),
            pl.BlockSpec(memory_space=pltpu.VMEM),
        ],
        scratch_shapes=[
            pltpu.SMEM((2 * count,), jnp.float32),
            pltpu.SMEM((slots, LANES), jnp.int32),
            pltpu.VMEM((slots * meta, LANES), jnp.float32),
            pltpu.VMEM((slots * meta, LANES), jnp.float32),
            pltpu.SMEM((slots * bins + 4 * TOGETHER,), jnp.int32),
            pltpu.VMEM(ztab.shape[1:], jnp.bfloat16),
            pltpu.VMEM(ytab.shape, jnp.bfloat16),
            pltpu.VMEM((XS, 2, block, NY), jnp.float32),
            pltpu.SemaphoreType.DMA((4,)),
            pltpu.SemaphoreType.DMA((XS,)),
        ]
        + [pltpu.VMEM((XS * PATCH, particles), jnp.bfloat16)] * (2 * TOGETHER)
        + [pltpu.VMEM((block + WINDOW, particles), jnp.float32)] * (2 * TOGETHER)
        + [pltpu.VMEM((PATCH, particles), jnp.float32)] * (2 * TOGETHER),
        out_shape=[
            jax.ShapeDtypeStruct((2, XS, block, NY), jnp.float32),
            jax.ShapeDtypeStruct((1, 1), jnp.float32),
            pltpu.VMEM((folded_rows, LANES), jnp.float32),
        ],
        input_output_aliases={1: 2},
        compiler_params=pltpu.CompilerParams(vmem_limit_bytes=36 * 1024 * 1024),
        name="spread_and_transform",
    )(
        pltpu.with_memory_space_constraint(parts, pltpu.VMEM),
        pltpu.with_memory_space_constraint(folded, pltpu.VMEM),
        in_hbm(ztab),
        in_hbm(ytab),
    )
    return (spectrum, load)


def solution(mesh):
    return jax.shard_map(
        body,
        mesh=mesh,
        in_specs=(
            P(("wide", "narrow"), None, None),
            P(("wide", "narrow"), None),
            P(("wide", "narrow")),
            P(None, ("wide", "narrow")),
            P(("wide", "narrow"), None),
        ),
        out_specs=(P(None, "wide", "narrow", None), P("wide", "narrow")),
        check_vma=False,
    )
```

```python
import math

import jax
import jax.numpy as jnp
import numpy as np
from jax import lax
from jax.experimental import pallas as pl
from jax.experimental.pallas import tpu as pltpu
from jax.sharding import PartitionSpec as P

XS = 8
NY = 1024
NZ = 1024
PATCH = 24
SPLIT = 8
WINDOW = 32
TOGETHER = 4
LANES = 128
PAIR = 2

LOWEST, SPAN = 6.0, 12.0
POSITION_STEPS = 65535.0
FORCE_STEPS = 32000.0
FORCE_ZERO = 32768

spread_rate = 0.08
spread_root = math.sqrt(spread_rate / math.log(2.0))
two_pi = 2.0 * math.pi


def y_tables():
    points = NY // SPLIT
    y = np.arange(points)[None, :] * SPLIT + np.arange(SPLIT)[:, None]
    phase = (y[:, :, None] * np.arange(points)[None, None, :]) % NY
    angle = phase * (two_pi / NY)
    cos = np.cos(angle) / math.sqrt(NY)
    sin = np.sin(angle) / math.sqrt(NY)
    upper = np.concatenate([cos, -sin], axis=2)
    lower = np.concatenate([sin, cos], axis=2)
    return np.concatenate([upper, lower], axis=1).astype(np.float32).astype(jnp.bfloat16)


def z_tables(block, count):
    frequency = np.arange(block)[None, :] * count + np.arange(count)[:, None]
    phase = frequency[:, :, None] * np.arange(block)[None, None, :] % NZ
    angle = phase * (two_pi / NZ)
    cos = np.cos(angle) / math.sqrt(NZ)
    sin = np.sin(angle) / math.sqrt(NZ)
    top = np.concatenate([cos, sin], axis=2)
    bottom = np.concatenate([-sin, cos], axis=2)
    return np.concatenate([top, bottom], axis=1).astype(np.float32).astype(jnp.bfloat16)


def turns(count):
    angle = np.arange(count) * (two_pi / count)
    return np.concatenate([np.cos(angle), -np.sin(angle)]).astype(np.float32)


def encode(positions, forces, counts, anchors, helpers, own, bins):
    particles = forces.shape[1]
    scale = POSITION_STEPS / SPAN

    def place(c):
        code = (positions[:, c, :] - LOWEST) * scale + 0.5
        return jnp.clip(code, 0.0, POSITION_STEPS).astype(jnp.int32)

    lane = lax.broadcasted_iota(jnp.int32, (bins, LANES), 1)
    bin_of = lax.broadcasted_iota(jnp.int32, (bins, LANES), 0)
    row = jnp.concatenate(
        [
            counts[...],
            anchors[0:1, :],
            anchors[1:2, :],
            anchors[2:3, :],
            helpers[...],
            jnp.zeros((1, LANES - 5 * bins), jnp.int32),
        ],
        axis=1,
    )
    spread_counts = jnp.broadcast_to(row.astype(jnp.float32), (bins, LANES))
    live = jnp.sum(jnp.where(lane == bin_of, spread_counts, 0.0), axis=1, keepdims=True)
    slot = lax.broadcasted_iota(jnp.int32, (bins, particles), 1).astype(jnp.float32)
    force = jnp.where(slot < live, forces[...], 0.0)
    largest = jnp.max(jnp.max(jnp.abs(force), axis=1, keepdims=True), axis=0, keepdims=True)
    power = jnp.ceil(jnp.log2(jnp.maximum(largest, 1e-36)))
    code = (force * jnp.exp2(-power) * FORCE_STEPS + (FORCE_ZERO + 0.5)).astype(jnp.int32)
    first = lax.shift_left(place(0), 16) | place(1)
    second = lax.shift_left(place(2), 16) | code
    for h in range(particles // LANES):
        own[h * bins : (h + 1) * bins, :] = first[:, h * LANES : (h + 1) * LANES]
    for h in range(particles // LANES):
        at = particles // LANES * bins + h * bins
        own[at : at + bins, :] = second[:, h * LANES : (h + 1) * LANES]
    at = 2 * particles // LANES * bins
    lane = lax.broadcasted_iota(jnp.int32, (1, LANES), 1)
    power = jnp.broadcast_to(power.astype(jnp.int32), (1, LANES))
    alive = jnp.where((lane < bins) & (row > 0), 1.0, 0.0)
    alive = jnp.sum(alive, axis=1, keepdims=True).astype(jnp.int32)
    row = jnp.where(lane == 5 * bins, power, row)
    own[at : at + 1, :] = jnp.where(lane == 5 * bins + 1, alive, row)


def gather_kernel(
    *refs, wide, count, slabs, stride
):
    given, refs = refs[:5], refs[5:]
    parts, folded, positions, forces, counts, anchors, helpers = refs[:7]
    block_own, send, receive, local, fetched = refs[7:]
    fetches = [
        pltpu.make_async_copy(source, target, fetched.at[i])
        for i, (source, target) in enumerate(zip(given, refs[2:7]))
    ]
    for fetch in fetches:
        fetch.start()
    w, n = lax.axis_index("wide"), lax.axis_index("narrow")
    chips = count // 2
    z, core = n // 2, n % 2
    other = z * 2 + (1 - core)

    used = 2 * forces.shape[1] // LANES * forces.shape[0] + 1

    def place(distance, index):
        return parts.at[distance * count + index, pl.ds(0, used)]

    def at(distance, index):
        return receive.at[distance * count + index]

    def later(distance):
        return (w + distance) % wide

    def across(step):
        chip, bit = z, 1
        while bit <= step:
            if step & bit:
                chip = chip + bit - 2 * bit * (z // bit % 2)
            bit *= 2
        return chip * 2 + core

    peers = [across(step) for step in range(1, chips)]
    barrier = pltpu.get_barrier_semaphore()
    for peer in peers[::-1] + [other]:
        pl.semaphore_signal(
            barrier, inc=1, device_id=(w, peer), device_id_type=pl.DeviceIdType.MESH
        )
    for distance in range(1, slabs):
        for target in (n, other):
            pl.semaphore_signal(
                barrier,
                inc=1,
                device_id=((w + wide - distance) % wide, target),
                device_id_type=pl.DeviceIdType.MESH,
            )
    own = block_own.at[pl.ds(0, used), :]
    for fetch in fetches:
        fetch.wait()
    encode(positions, forces, counts, anchors, helpers, block_own, forces.shape[0])
    pl.semaphore_wait(barrier, chips + 2 * (slabs - 1))

    sent = []

    def push(source, target, distance, index):
        copy = pltpu.make_async_remote_copy(
            src_ref=source,
            dst_ref=place(distance, index),
            send_sem=send.at[len(sent)],
            recv_sem=at(distance, index),
            device_id=target,
            device_id_type=pl.DeviceIdType.MESH,
        )
        copy.start()
        sent.append(copy)

    def arrived(distance, index):
        pltpu.make_async_remote_copy(
            src_ref=own,
            dst_ref=place(distance, index),
            send_sem=send.at[0],
            recv_sem=at(distance, index),
            device_id=(w, other),
            device_id_type=pl.DeviceIdType.MESH,
        ).wait_recv()

    for peer in peers[::-1]:
        push(own, (w, peer), 0, n)
    for distance in range(1, slabs):
        push(own, (later(distance), n), distance, n)
    push(own, (w, other), 0, n)
    keep = pltpu.make_async_copy(own, place(0, n), local)
    keep.start()
    sources = [n] + peers
    last = (chips - 1,)
    zero_rows = folded.shape[0] // (slabs * count)

    def clear(i, carry):
        at_row = pl.multiple_of(i * zero_rows, 8)
        folded[pl.ds(at_row, zero_rows), :] = jnp.zeros((zero_rows, LANES), jnp.float32)
        return carry

    lax.fori_loop(0, slabs * count, clear, 0)
    for index, source in list(enumerate(sources))[1:]:
        arrived(0, source)
        for distance in range(1, slabs):
            push(place(0, source), (later(distance), n), distance, source)
        push(place(0, source), (w, other), 0, source)
        if index in last:
            for distance in range(1, slabs):
                push(place(0, source), (later(distance), other), distance, source)
    for index, source in enumerate(sources):
        for distance in range(1, slabs):
            arrived(distance, source)
            if index not in last:
                push(place(distance, source), (w, other), distance, source)
    for distance in range(slabs):
        for chip in range(chips):
            arrived(distance, chip * 2 + (1 - core))
    for copy in sent:
        copy.wait_send()
    keep.wait()


def spectrum_kernel(
    coded, _, ztab_hbm, ytab_hbm, out, load, folded, turn, facts, upper, lower, items,
    ztab, ytab, results, sems, sent, *work,
    bins, block, count, own_rows, slabs
):
    lefts, helds, acrosses = (work[i * 2 * TOGETHER : (i + 1) * 2 * TOGETHER] for i in range(3))
    me = lax.axis_index("narrow")
    slots = slabs * count
    halves = lefts[0].shape[1] // LANES
    count_bits = count.bit_length() - 1
    block_bits = block.bit_length() - 1
    particles = halves * LANES
    half_rows = halves * bins
    meta = 2 * half_rows
    folds = 2 * block // LANES
    step = SPLIT + 1
    pitch = ((NY + WINDOW) // SPLIT * step + slots - 1) // slots * slots
    points = NY // SPLIT

    to_smem = pltpu.make_async_copy(coded.at[:, meta, :], facts, sems.at[0])
    z_copy = pltpu.make_async_copy(ztab_hbm.at[me], ztab, sems.at[2])
    y_copy = pltpu.make_async_copy(ytab_hbm, ytab, sems.at[3])
    to_smem.start()
    z_copy.start()
    y_copy.start()
    for i, part in enumerate(turns(count)):
        turn[i] = jnp.float32(float(part))

    home = jnp.concatenate([coded[d, meta : meta + 1, :] for d in range(count)], axis=0)
    helper = pltpu.roll(home, LANES - 4 * bins, axis=1)
    lane = lax.broadcasted_iota(jnp.int32, home.shape, 1)
    mine = jnp.where((lane < bins) & (helper == me), home, 0).astype(jnp.float32)
    load[...] = jnp.sum(mine, keepdims=True).reshape(1, 1) / particles

    def decode(device):
        power = coded[device, meta : meta + 1, 5 * bins : 5 * bins + 1].astype(jnp.float32)
        gain = jnp.exp2(power) * (1.0 / FORCE_STEPS)
        word = coded[device, :meta, :]
        high = lax.shift_right_logical(word, 16).astype(jnp.float32)
        low = (word & 65535).astype(jnp.float32)
        unit = SPAN / POSITION_STEPS * spread_root
        at_row = pl.multiple_of(device * meta, 8)
        upper[pl.ds(at_row, meta), :] = high * unit + LOWEST * spread_root
        lower[pl.ds(at_row, half_rows), :] = low[:half_rows] * unit + LOWEST * spread_root
        lower[pl.ds(pl.multiple_of(at_row + half_rows, 8), half_rows), :] = (
            low[half_rows:] - FORCE_ZERO
        ) * gain

    def decode_some(i, carry):
        for k in range(4):
            decode(4 * i + k)
        return carry

    lax.fori_loop(0, slots // 4, decode_some, 0)
    to_smem.wait()

    def collect(i, total):
        for k in range(4):
            device = 4 * i + k
            for b in range(bins):
                items[total + b] = device * 16 + b
            total = total + facts[device, 5 * bins + 1]
        return total

    total = lax.fori_loop(0, slots // 4, collect, 0)
    for extra in range(4 * TOGETHER):
        items[total + extra] = 0

    cell = lax.broadcasted_iota(jnp.int32, (8, particles), 0)
    steps8 = cell.astype(jnp.float32) * spread_root

    def gauss(first, place):
        away = (steps8 + first * spread_root) - place
        return jnp.exp2(-(away * away))

    def line(ref, row):
        return jnp.concatenate([ref[pl.ds(row + h * bins, 1), :] for h in range(halves)], axis=1)

    def build(k, left, held, across):
        item = items[k]
        device, b = item >> 4, item & 15
        r = device * meta + b
        x0 = (device >> count_bits) * XS - facts[device, bins + b]
        shift = facts[device, 3 * bins + b] & 7
        at = pl.multiple_of(facts[device, 3 * bins + b] & (block - 8), 8)
        px = line(upper, r) - x0.astype(jnp.float32) * spread_root
        py = line(lower, r)
        pz = line(upper, r + half_rows) + shift.astype(jnp.float32) * spread_root
        force = line(lower, r + half_rows)
        force = jnp.where(k < total, force, jnp.zeros_like(force))
        along_x = gauss(0, px) * force
        along_x = jnp.where((cell >= -x0) & (cell < PATCH - x0), along_x, 0.0)
        along_x = jnp.concatenate([along_x, along_x], axis=0).astype(jnp.bfloat16)
        for i in range(PATCH // 8):
            across[8 * i : 8 * i + 8, :] = gauss(8 * i, py)
        for j in range(0, PATCH, 2):
            one = [jnp.broadcast_to(across[j + i : j + i + 1, :], (8, particles)) for i in range(2)]
            one = jnp.concatenate(one, axis=0).astype(jnp.bfloat16)
            left[XS * j : XS * (j + 2), :] = along_x * one
        along_z = [gauss(8 * i, pz) for i in range(4)]
        along_z[0] = jnp.where(cell >= shift, along_z[0], 0.0)
        along_z[3] = jnp.where(cell < shift, along_z[3], 0.0)
        held[pl.ds(at, WINDOW), :] = jnp.concatenate(along_z, axis=0)

    lane = lax.broadcasted_iota(jnp.int32, (1, LANES), 1)

    def settle(k, left, held):
        item = items[k]
        device, b = item >> 4, item & 15
        y0 = (device & (count - 1)) * own_rows + facts[device, 2 * bins + b]
        z0 = facts[device, 3 * bins + b]
        at = pl.multiple_of(z0 & (block - 8), 8)
        turned = (z0 >> block_bits) * me
        s0 = turned & (count - 1)
        s1 = (turned + me) & (count - 1)
        right = jnp.concatenate(
            [held[:WINDOW, :] + held[block:, :], held[WINDOW:block, :]], axis=0
        ).astype(jnp.bfloat16)
        held[pl.ds(at, WINDOW), :] = jnp.zeros((WINDOW, particles), jnp.float32)
        value = lax.dot_general(
            left[...],
            jnp.concatenate([right] * (LANES // block), axis=0),
            (((1,), (1,)), ((), ())),
            preferred_element_type=jnp.float32,
        )
        factors = []
        for h in range(folds):
            spot = lane + h * LANES
            wrapped = (spot & (block - 1)) < at
            factor = jnp.where(
                spot < block,
                jnp.where(wrapped, turn[s1], turn[s0]),
                jnp.where(wrapped, turn[count + s1], turn[count + s0]),
            )
            factors.append(factor)
        base = y0 + (y0 >> 3)
        spots = []
        for i in range(PATCH // SPLIT):
            for j in range(SPLIT):
                first = base + jnp.where((y0 & 7) + j >= SPLIT, j + 1, j)
                spots.append([pl.multiple_of((first + (h * pitch + i * step)) * XS, 8) for h in range(folds)])
        olds = [[folded[pl.ds(spot[h], XS), :] for h in range(folds)] for spot in spots]
        for j, spot in enumerate(spots):
            for h in range(folds):
                one = value[j * XS : (j + 1) * XS, :]
                folded[pl.ds(spot[h], XS), :] = olds[j][h] + one * factors[h]

    for held in helds:
        held[...] = jnp.zeros_like(held)
    for u in range(TOGETHER):
        build(u, lefts[u], helds[u], acrosses[u])

    def group(g, carry):
        for half in range(2):
            here, there = half * TOGETHER, (1 - half) * TOGETHER
            k = (2 * g + half) * TOGETHER
            for u in range(TOGETHER):
                build(
                    k + TOGETHER + u, lefts[there + u], helds[there + u], acrosses[there + u]
                )
                settle(k + u, lefts[here + u], helds[here + u])
        return carry

    lax.fori_loop(0, (total + 2 * TOGETHER - 1) // (2 * TOGETHER), group, 0)
    for h in range(folds):
        at_row = h * pitch * XS
        over = at_row + NY // SPLIT * step * XS
        rows = PATCH // SPLIT * step * XS
        folded[at_row : at_row + rows, :] += folded[over : over + rows, :]
    z_copy.wait()
    y_copy.wait()

    terms = {}

    def transform(pair, t):
        lines = jnp.concatenate(
            [
                jnp.concatenate(
                    [
                        folded[
                            pl.ds((h * pitch + t) * XS + pair * PAIR + x, points, stride=step * XS), :
                        ].astype(jnp.bfloat16)
                        for h in range(folds)
                    ],
                    axis=1,
                )
                for x in range(PAIR)
            ],
            axis=0,
        )
        along = lax.dot_general(
            ztab[...], lines, (((1,), (1,)), ((), ())), preferred_element_type=jnp.float32
        ).astype(jnp.bfloat16)
        along = jnp.concatenate(
            [
                jnp.concatenate(
                    [
                        along[:block, x * points : (x + 1) * points],
                        along[block:, x * points : (x + 1) * points],
                    ],
                    axis=1,
                )
                for x in range(PAIR)
            ],
            axis=0,
        )
        terms[pair % 2, t] = jnp.dot(along, ytab[t], preferred_element_type=jnp.float32)

    root = math.sqrt(0.5)

    def four(a, b, c, d):
        (ar, ai), (br, bi), (cr, ci), (dr, di) = a, b, c, d
        pr, pi, mr, mi = ar + cr, ai + ci, ar - cr, ai - ci
        qr, qi, nr, ni = br + dr, bi + di, br - dr, bi - di
        return (pr + qr, pi + qi), (mr + ni, mi - nr), (pr - qr, pi - qi), (mr - ni, mi + nr)

    def combine(pair, x, r):
        at_row = x * block + r
        term = [
            (
                terms[pair % 2, t][at_row : at_row + 8, :points],
                terms[pair % 2, t][at_row : at_row + 8, points:],
            )
            for t in range(SPLIT)
        ]
        even = four(term[0], term[2], term[4], term[6])
        odd = four(term[1], term[3], term[5], term[7])
        o1 = ((odd[1][0] + odd[1][1]) * root, (odd[1][1] - odd[1][0]) * root)
        o2 = (odd[2][1], -odd[2][0])
        o3 = ((odd[3][1] - odd[3][0]) * root, (odd[3][0] + odd[3][1]) * -root)
        slot = pair * PAIR + x
        for q, turned in enumerate((odd[0], o1, o2, o3)):
            for c in range(2):
                results[slot, c, r : r + 8, q * points : (q + 1) * points] = even[q][c] + turned[c]
                results[slot, c, r : r + 8, (q + 4) * points : (q + 5) * points] = (
                    even[q][c] - turned[c]
                )

    def leave(plane):
        return pltpu.make_async_copy(
            results.at[plane], out.at[:, plane], sent.at[plane]
        )

    pairs = XS // PAIR
    todo = [(x, r) for x in range(PAIR) for r in range(0, block, 8)]
    each = len(todo) // SPLIT
    for pair in range(pairs):
        for t in range(SPLIT):
            transform(pair, t)
        for t in range(SPLIT):
            for x, r in todo[t * each : (t + 1) * each]:
                plane = pair * PAIR + x
                combine(pair, x, r)
                if r + 8 == block:
                    leave(plane).start()
    for plane in range(XS):
        leave(plane).wait()


def in_hbm(x):
    return pltpu.with_memory_space_constraint(x, pltpu.HBM)


def body(positions, forces, counts, anchors, helpers):
    bins, _, particles = positions.shape
    count = lax.axis_size("narrow")
    wide = lax.axis_size("wide")
    me = lax.axis_index("narrow")
    block = NZ // count
    own_rows = NY // count
    slabs = 1 + (PATCH + XS - 2) // XS
    slots = slabs * count
    stride = (2 * particles // LANES * bins + 1 + 7) // 8 * 8

    pitch = ((NY + WINDOW) // SPLIT * (SPLIT + 1) + slots - 1) // slots * slots
    folded_rows = 2 * block // LANES * pitch * XS
    parts, folded = pl.pallas_call(
        lambda *refs: gather_kernel(*refs, wide=wide, count=count, slabs=slabs, stride=stride),
        in_specs=[pl.BlockSpec(memory_space=pl.ANY)] * 5,
        out_specs=[pl.BlockSpec(memory_space=pl.ANY), pl.BlockSpec(memory_space=pltpu.VMEM)],
        out_shape=[
            pltpu.VMEM((slots, stride, LANES), jnp.int32),
            pltpu.VMEM((folded_rows, LANES), jnp.float32),
        ],
        scratch_shapes=[
            pltpu.VMEM(positions.shape, jnp.float32),
            pltpu.VMEM(forces.shape, jnp.float32),
            pltpu.VMEM((1, bins), jnp.int32),
            pltpu.VMEM(anchors.shape, jnp.int32),
            pltpu.VMEM((1, bins), jnp.int32),
            pltpu.VMEM((stride, LANES), jnp.int32),
            pltpu.SemaphoreType.DMA((slots,)),
            pltpu.SemaphoreType.DMA((slots,)),
            pltpu.SemaphoreType.DMA,
            pltpu.SemaphoreType.DMA((5,)),
        ],
        compiler_params=pltpu.CompilerParams(
            collective_id=0, has_side_effects=True, vmem_limit_bytes=16 * 1024 * 1024
        ),
        name="gather_particles",
    )(*map(in_hbm, (positions, forces, counts.reshape(1, bins), anchors, helpers.reshape(1, bins))))
    ytab = jnp.asarray(y_tables())
    ztab = jnp.asarray(z_tables(block, count))
    meta = 2 * particles // LANES * bins

    spectrum, load, _ = pl.pallas_call(
        lambda *refs: spectrum_kernel(
            *refs, bins=bins, block=block, count=count, own_rows=own_rows, slabs=slabs
        ),
        in_specs=[pl.BlockSpec(memory_space=pltpu.VMEM)] * 2
        + [pl.BlockSpec(memory_space=pl.ANY)] * 2,
        out_specs=[
            pl.BlockSpec(memory_space=pl.ANY),
            pl.BlockSpec(memory_space=pltpu.VMEM),
            pl.BlockSpec(memory_space=pltpu.VMEM),
        ],
        scratch_shapes=[
            pltpu.SMEM((2 * count,), jnp.float32),
            pltpu.SMEM((slots, LANES), jnp.int32),
            pltpu.VMEM((slots * meta, LANES), jnp.float32),
            pltpu.VMEM((slots * meta, LANES), jnp.float32),
            pltpu.SMEM((slots * bins + 4 * TOGETHER,), jnp.int32),
            pltpu.VMEM(ztab.shape[1:], jnp.bfloat16),
            pltpu.VMEM(ytab.shape, jnp.bfloat16),
            pltpu.VMEM((XS, 2, block, NY), jnp.float32),
            pltpu.SemaphoreType.DMA((4,)),
            pltpu.SemaphoreType.DMA((XS,)),
        ]
        + [pltpu.VMEM((XS * PATCH, particles), jnp.bfloat16)] * (2 * TOGETHER)
        + [pltpu.VMEM((block + WINDOW, particles), jnp.float32)] * (2 * TOGETHER)
        + [pltpu.VMEM((PATCH, particles), jnp.float32)] * (2 * TOGETHER),
        out_shape=[
            jax.ShapeDtypeStruct((2, XS, block, NY), jnp.float32),
            jax.ShapeDtypeStruct((1, 1), jnp.float32),
            pltpu.VMEM((folded_rows, LANES), jnp.float32),
        ],
        input_output_aliases={1: 2},
        compiler_params=pltpu.CompilerParams(vmem_limit_bytes=36 * 1024 * 1024),
        name="spread_and_transform",
    )(
        pltpu.with_memory_space_constraint(parts, pltpu.VMEM),
        pltpu.with_memory_space_constraint(folded, pltpu.VMEM),
        in_hbm(ztab),
        in_hbm(ytab),
    )
    return (spectrum, load)


def solution(mesh):
    return jax.shard_map(
        body,
        mesh=mesh,
        in_specs=(
            P(("wide", "narrow"), None, None),
            P(("wide", "narrow"), None),
            P(("wide", "narrow")),
            P(None, ("wide", "narrow")),
            P(("wide", "narrow"), None),
        ),
        out_specs=(P(None, "wide", "narrow", None), P("wide", "narrow")),
        check_vma=False,
    )
```

```python
import math

import jax
import jax.numpy as jnp
import numpy as np
from jax import lax
from jax.experimental import pallas as pl
from jax.experimental.pallas import tpu as pltpu
from jax.sharding import PartitionSpec as P

XS = 8
NY = 1024
NZ = 1024
PATCH = 24
SPLIT = 8
WINDOW = 32
TOGETHER = 4
LANES = 128
PAIR = 2

LOWEST, SPAN = 6.0, 12.0
POSITION_STEPS = 65535.0
FORCE_STEPS = 32000.0
FORCE_ZERO = 32768

spread_rate = 0.08
spread_root = math.sqrt(spread_rate / math.log(2.0))
two_pi = 2.0 * math.pi


def y_tables():
    points = NY // SPLIT
    y = np.arange(points)[None, :] * SPLIT + np.arange(SPLIT)[:, None]
    phase = (y[:, :, None] * np.arange(points)[None, None, :]) % NY
    angle = phase * (two_pi / NY)
    cos = np.cos(angle) / math.sqrt(NY)
    sin = np.sin(angle) / math.sqrt(NY)
    upper = np.concatenate([cos, -sin], axis=2)
    lower = np.concatenate([sin, cos], axis=2)
    return np.concatenate([upper, lower], axis=1).astype(np.float32).astype(jnp.bfloat16)


def z_tables(block, count):
    frequency = np.arange(block)[None, :] * count + np.arange(count)[:, None]
    phase = frequency[:, :, None] * np.arange(block)[None, None, :] % NZ
    angle = phase * (two_pi / NZ)
    cos = np.cos(angle) / math.sqrt(NZ)
    sin = np.sin(angle) / math.sqrt(NZ)
    top = np.concatenate([cos, sin], axis=2)
    bottom = np.concatenate([-sin, cos], axis=2)
    return np.concatenate([top, bottom], axis=1).astype(np.float32).astype(jnp.bfloat16)


def turns(count):
    angle = np.arange(count) * (two_pi / count)
    return np.concatenate([np.cos(angle), -np.sin(angle)]).astype(np.float32)


def encode(positions, forces, counts, anchors, helpers, own, bins):
    particles = forces.shape[1]
    scale = POSITION_STEPS / SPAN

    def place(c):
        code = (positions[:, c, :] - LOWEST) * scale + 0.5
        return jnp.clip(code, 0.0, POSITION_STEPS).astype(jnp.int32)

    lane = lax.broadcasted_iota(jnp.int32, (bins, LANES), 1)
    bin_of = lax.broadcasted_iota(jnp.int32, (bins, LANES), 0)
    row = jnp.concatenate(
        [
            counts[...],
            anchors[0:1, :],
            anchors[1:2, :],
            anchors[2:3, :],
            helpers[...],
            jnp.zeros((1, LANES - 5 * bins), jnp.int32),
        ],
        axis=1,
    )
    spread_counts = jnp.broadcast_to(row.astype(jnp.float32), (bins, LANES))
    live = jnp.sum(jnp.where(lane == bin_of, spread_counts, 0.0), axis=1, keepdims=True)
    slot = lax.broadcasted_iota(jnp.int32, (bins, particles), 1).astype(jnp.float32)
    force = jnp.where(slot < live, forces[...], 0.0)
    largest = jnp.max(jnp.max(jnp.abs(force), axis=1, keepdims=True), axis=0, keepdims=True)
    power = jnp.ceil(jnp.log2(jnp.maximum(largest, 1e-36)))
    code = (force * jnp.exp2(-power) * FORCE_STEPS + (FORCE_ZERO + 0.5)).astype(jnp.int32)
    first = lax.shift_left(place(0), 16) | place(1)
    second = lax.shift_left(place(2), 16) | code
    for h in range(particles // LANES):
        own[h * bins : (h + 1) * bins, :] = first[:, h * LANES : (h + 1) * LANES]
    for h in range(particles // LANES):
        at = particles // LANES * bins + h * bins
        own[at : at + bins, :] = second[:, h * LANES : (h + 1) * LANES]
    at = 2 * particles // LANES * bins
    lane = lax.broadcasted_iota(jnp.int32, (1, LANES), 1)
    power = jnp.broadcast_to(power.astype(jnp.int32), (1, LANES))
    alive = jnp.where((lane < bins) & (row > 0), 1.0, 0.0)
    alive = jnp.sum(alive, axis=1, keepdims=True).astype(jnp.int32)
    row = jnp.where(lane == 5 * bins, power, row)
    own[at : at + 1, :] = jnp.where(lane == 5 * bins + 1, alive, row)


def gather_kernel(
    *refs, wide, count, slabs, stride
):
    given, refs = refs[:5], refs[5:]
    parts, folded, positions, forces, counts, anchors, helpers = refs[:7]
    block_own, send, receive, local, fetched = refs[7:]
    fetches = [
        pltpu.make_async_copy(source, target, fetched.at[i])
        for i, (source, target) in enumerate(zip(given, refs[2:7]))
    ]
    for fetch in fetches:
        fetch.start()
    w, n = lax.axis_index("wide"), lax.axis_index("narrow")
    chips = count // 2
    z, core = n // 2, n % 2
    other = z * 2 + (1 - core)

    used = 2 * forces.shape[1] // LANES * forces.shape[0] + 1

    def place(distance, index):
        return parts.at[distance * count + index, pl.ds(0, used)]

    def at(distance, index):
        return receive.at[distance * count + index]

    def later(distance):
        return (w + distance) % wide

    def across(step):
        chip, bit = z, 1
        while bit <= step:
            if step & bit:
                chip = chip + bit - 2 * bit * (z // bit % 2)
            bit *= 2
        return chip * 2 + core

    peers = [across(step) for step in range(1, chips)]
    barrier = pltpu.get_barrier_semaphore()
    for peer in peers[::-1] + [other]:
        pl.semaphore_signal(
            barrier, inc=1, device_id=(w, peer), device_id_type=pl.DeviceIdType.MESH
        )
    for distance in range(1, slabs):
        for target in (n, other):
            pl.semaphore_signal(
                barrier,
                inc=1,
                device_id=((w + wide - distance) % wide, target),
                device_id_type=pl.DeviceIdType.MESH,
            )
    own = block_own.at[pl.ds(0, used), :]
    for fetch in fetches:
        fetch.wait()
    encode(positions, forces, counts, anchors, helpers, block_own, forces.shape[0])
    pl.semaphore_wait(barrier, chips + 2 * (slabs - 1))

    sent = []

    def push(source, target, distance, index):
        copy = pltpu.make_async_remote_copy(
            src_ref=source,
            dst_ref=place(distance, index),
            send_sem=send.at[len(sent)],
            recv_sem=at(distance, index),
            device_id=target,
            device_id_type=pl.DeviceIdType.MESH,
        )
        copy.start()
        sent.append(copy)

    def arrived(distance, index):
        pltpu.make_async_remote_copy(
            src_ref=own,
            dst_ref=place(distance, index),
            send_sem=send.at[0],
            recv_sem=at(distance, index),
            device_id=(w, other),
            device_id_type=pl.DeviceIdType.MESH,
        ).wait_recv()

    for peer in peers[::-1]:
        push(own, (w, peer), 0, n)
    for distance in range(1, slabs):
        push(own, (later(distance), n), distance, n)
    push(own, (w, other), 0, n)
    keep = pltpu.make_async_copy(own, place(0, n), local)
    keep.start()
    sources = [n] + peers
    last = (chips - 1,)
    zero_rows = folded.shape[0] // (slabs * count)

    def clear(i, carry):
        at_row = pl.multiple_of(i * zero_rows, 8)
        folded[pl.ds(at_row, zero_rows), :] = jnp.zeros((zero_rows, LANES), jnp.float32)
        return carry

    lax.fori_loop(0, slabs * count, clear, 0)
    for index, source in list(enumerate(sources))[1:]:
        arrived(0, source)
        for distance in range(1, slabs):
            push(place(0, source), (later(distance), n), distance, source)
        push(place(0, source), (w, other), 0, source)
        if index in last:
            for distance in range(1, slabs):
                push(place(0, source), (later(distance), other), distance, source)
    for index, source in enumerate(sources):
        for distance in range(1, slabs):
            arrived(distance, source)
            if index not in last:
                push(place(distance, source), (w, other), distance, source)
    keep.wait()
    for copy in sent[: 1 - slabs]:
        copy.wait_send()
    for distance in range(slabs):
        for chip in range(chips):
            arrived(distance, chip * 2 + (1 - core))
    for copy in sent[1 - slabs :]:
        copy.wait_send()


def spectrum_kernel(
    coded, _, ztab_hbm, ytab_hbm, out, load_hbm, folded, load, turn, facts, upper, lower, items,
    ztab, ytab, results, sems, sent, *work,
    bins, block, count, own_rows, slabs
):
    lefts, helds, acrosses = (work[i * 2 * TOGETHER : (i + 1) * 2 * TOGETHER] for i in range(3))
    me = lax.axis_index("narrow")
    slots = slabs * count
    halves = lefts[0].shape[1] // LANES
    count_bits = count.bit_length() - 1
    block_bits = block.bit_length() - 1
    particles = halves * LANES
    half_rows = halves * bins
    meta = 2 * half_rows
    folds = 2 * block // LANES
    step = SPLIT + 1
    pitch = ((NY + WINDOW) // SPLIT * step + slots - 1) // slots * slots
    points = NY // SPLIT

    to_smem = pltpu.make_async_copy(coded.at[:, meta, :], facts, sems.at[0])
    z_copy = pltpu.make_async_copy(ztab_hbm.at[me], ztab, sems.at[2])
    y_copy = pltpu.make_async_copy(ytab_hbm, ytab, sems.at[3])
    to_smem.start()
    z_copy.start()
    y_copy.start()
    for i, part in enumerate(turns(count)):
        turn[i] = jnp.float32(float(part))

    home = jnp.concatenate([coded[d, meta : meta + 1, :] for d in range(count)], axis=0)
    helper = pltpu.roll(home, LANES - 4 * bins, axis=1)
    lane = lax.broadcasted_iota(jnp.int32, home.shape, 1)
    mine = jnp.where((lane < bins) & (helper == me), home, 0).astype(jnp.float32)
    load[...] = jnp.sum(mine, keepdims=True).reshape(1, 1) / particles
    load_copy = pltpu.make_async_copy(load, load_hbm, sems.at[1])
    load_copy.start()

    def decode(device):
        power = coded[device, meta : meta + 1, 5 * bins : 5 * bins + 1].astype(jnp.float32)
        gain = jnp.exp2(power) * (1.0 / FORCE_STEPS)
        word = coded[device, :meta, :]
        high = lax.shift_right_logical(word, 16).astype(jnp.float32)
        low = (word & 65535).astype(jnp.float32)
        unit = SPAN / POSITION_STEPS * spread_root
        at_row = pl.multiple_of(device * meta, 8)
        upper[pl.ds(at_row, meta), :] = high * unit + LOWEST * spread_root
        lower[pl.ds(at_row, half_rows), :] = low[:half_rows] * unit + LOWEST * spread_root
        lower[pl.ds(pl.multiple_of(at_row + half_rows, 8), half_rows), :] = (
            low[half_rows:] - FORCE_ZERO
        ) * gain

    def decode_some(i, carry):
        for k in range(4):
            decode(4 * i + k)
        return carry

    lax.fori_loop(0, slots // 4, decode_some, 0)
    to_smem.wait()

    def collect(i, total):
        alive = [facts[8 * i + k, 5 * bins + 1] for k in range(8)]
        for k in range(8):
            for b in range(bins):
                items[total + b] = (8 * i + k) * 16 + b
            total = total + alive[k]
        return total

    total = lax.fori_loop(0, slots // 8, collect, 0)
    for extra in range(4 * TOGETHER):
        items[total + extra] = 0

    cell = lax.broadcasted_iota(jnp.int32, (8, particles), 0)
    steps8 = cell.astype(jnp.float32) * spread_root

    def gauss(first, place):
        away = (steps8 + first * spread_root) - place
        return jnp.exp2(-(away * away))

    def line(ref, row):
        return jnp.concatenate([ref[pl.ds(row + h * bins, 1), :] for h in range(halves)], axis=1)

    def build(k, left, held, across):
        item = items[k]
        device, b = item >> 4, item & 15
        r = device * meta + b
        x0 = (device >> count_bits) * XS - facts[device, bins + b]
        shift = facts[device, 3 * bins + b] & 7
        at = pl.multiple_of(facts[device, 3 * bins + b] & (block - 8), 8)
        px = line(upper, r) - x0.astype(jnp.float32) * spread_root
        py = line(lower, r)
        pz = line(upper, r + half_rows) + shift.astype(jnp.float32) * spread_root
        force = line(lower, r + half_rows)
        force = jnp.where(k < total, force, jnp.zeros_like(force))
        along_x = gauss(0, px) * force
        along_x = jnp.where((cell >= -x0) & (cell < PATCH - x0), along_x, 0.0)
        along_x = jnp.concatenate([along_x, along_x], axis=0).astype(jnp.bfloat16)
        for i in range(PATCH // 8):
            across[8 * i : 8 * i + 8, :] = gauss(8 * i, py)
        for j in range(0, PATCH, 2):
            one = [jnp.broadcast_to(across[j + i : j + i + 1, :], (8, particles)) for i in range(2)]
            one = jnp.concatenate(one, axis=0).astype(jnp.bfloat16)
            left[XS * j : XS * (j + 2), :] = along_x * one
        along_z = [gauss(8 * i, pz) for i in range(4)]
        along_z[0] = jnp.where(cell >= shift, along_z[0], 0.0)
        along_z[3] = jnp.where(cell < shift, along_z[3], 0.0)
        held[pl.ds(at, WINDOW), :] = jnp.concatenate(along_z, axis=0)

    lane = lax.broadcasted_iota(jnp.int32, (1, LANES), 1)

    def settle(k, left, held):
        item = items[k]
        device, b = item >> 4, item & 15
        y0 = (device & (count - 1)) * own_rows + facts[device, 2 * bins + b]
        z0 = facts[device, 3 * bins + b]
        at = pl.multiple_of(z0 & (block - 8), 8)
        turned = (z0 >> block_bits) * me
        s0 = turned & (count - 1)
        s1 = (turned + me) & (count - 1)
        right = jnp.concatenate(
            [held[:WINDOW, :] + held[block:, :], held[WINDOW:block, :]], axis=0
        ).astype(jnp.bfloat16)
        held[pl.ds(at, WINDOW), :] = jnp.zeros((WINDOW, particles), jnp.float32)
        value = lax.dot_general(
            left[...],
            jnp.concatenate([right] * (LANES // block), axis=0),
            (((1,), (1,)), ((), ())),
            preferred_element_type=jnp.float32,
        )
        factors = []
        for h in range(folds):
            spot = lane + h * LANES
            wrapped = (spot & (block - 1)) < at
            factor = jnp.where(
                spot < block,
                jnp.where(wrapped, turn[s1], turn[s0]),
                jnp.where(wrapped, turn[count + s1], turn[count + s0]),
            )
            factors.append(factor)
        base = y0 + (y0 >> 3)
        spots = []
        for i in range(PATCH // SPLIT):
            for j in range(SPLIT):
                first = base + jnp.where((y0 & 7) + j >= SPLIT, j + 1, j)
                spots.append([pl.multiple_of((first + (h * pitch + i * step)) * XS, 8) for h in range(folds)])
        olds = [[folded[pl.ds(spot[h], XS), :] for h in range(folds)] for spot in spots]
        for j, spot in enumerate(spots):
            for h in range(folds):
                one = value[j * XS : (j + 1) * XS, :]
                folded[pl.ds(spot[h], XS), :] = olds[j][h] + one * factors[h]

    for held in helds:
        held[...] = jnp.zeros_like(held)
    for u in range(TOGETHER):
        build(u, lefts[u], helds[u], acrosses[u])

    def group(g, carry):
        for half in range(2):
            here, there = half * TOGETHER, (1 - half) * TOGETHER
            k = (2 * g + half) * TOGETHER
            for u in range(TOGETHER):
                build(
                    k + TOGETHER + u, lefts[there + u], helds[there + u], acrosses[there + u]
                )
                settle(k + u, lefts[here + u], helds[here + u])
        return carry

    lax.fori_loop(0, (total + 2 * TOGETHER - 1) // (2 * TOGETHER), group, 0)
    for h in range(folds):
        at_row = h * pitch * XS
        over = at_row + NY // SPLIT * step * XS
        rows = PATCH // SPLIT * step * XS
        folded[at_row : at_row + rows, :] += folded[over : over + rows, :]
    z_copy.wait()
    y_copy.wait()

    terms = {}

    def transform(pair, t):
        lines = jnp.concatenate(
            [
                jnp.concatenate(
                    [
                        folded[
                            pl.ds((h * pitch + t) * XS + pair * PAIR + x, points, stride=step * XS), :
                        ].astype(jnp.bfloat16)
                        for h in range(folds)
                    ],
                    axis=1,
                )
                for x in range(PAIR)
            ],
            axis=0,
        )
        along = lax.dot_general(
            ztab[...], lines, (((1,), (1,)), ((), ())), preferred_element_type=jnp.float32
        ).astype(jnp.bfloat16)
        along = jnp.concatenate(
            [
                jnp.concatenate(
                    [
                        along[:block, x * points : (x + 1) * points],
                        along[block:, x * points : (x + 1) * points],
                    ],
                    axis=1,
                )
                for x in range(PAIR)
            ],
            axis=0,
        )
        terms[pair % 2, t] = jnp.dot(along, ytab[t], preferred_element_type=jnp.float32)

    root = math.sqrt(0.5)

    def four(a, b, c, d):
        (ar, ai), (br, bi), (cr, ci), (dr, di) = a, b, c, d
        pr, pi, mr, mi = ar + cr, ai + ci, ar - cr, ai - ci
        qr, qi, nr, ni = br + dr, bi + di, br - dr, bi - di
        return (pr + qr, pi + qi), (mr + ni, mi - nr), (pr - qr, pi - qi), (mr - ni, mi + nr)

    def combine(pair, x, r):
        at_row = x * block + r
        term = [
            (
                terms[pair % 2, t][at_row : at_row + 8, :points],
                terms[pair % 2, t][at_row : at_row + 8, points:],
            )
            for t in range(SPLIT)
        ]
        even = four(term[0], term[2], term[4], term[6])
        odd = four(term[1], term[3], term[5], term[7])
        o1 = ((odd[1][0] + odd[1][1]) * root, (odd[1][1] - odd[1][0]) * root)
        o2 = (odd[2][1], -odd[2][0])
        o3 = ((odd[3][1] - odd[3][0]) * root, (odd[3][0] + odd[3][1]) * -root)
        slot = pair * PAIR + x
        for q, turned in enumerate((odd[0], o1, o2, o3)):
            for c in range(2):
                results[slot, c, r : r + 8, q * points : (q + 1) * points] = even[q][c] + turned[c]
                results[slot, c, r : r + 8, (q + 4) * points : (q + 5) * points] = (
                    even[q][c] - turned[c]
                )

    def leave(plane):
        return pltpu.make_async_copy(
            results.at[plane], out.at[:, plane], sent.at[plane]
        )

    pairs = XS // PAIR
    todo = [(x, r) for x in range(PAIR) for r in range(0, block, 8)]
    each = len(todo) // SPLIT
    for pair in range(pairs):
        for t in range(SPLIT):
            transform(pair, t)
        for t in range(SPLIT):
            for x, r in todo[t * each : (t + 1) * each]:
                plane = pair * PAIR + x
                combine(pair, x, r)
                if r + 8 == block:
                    leave(plane).start()
    load_copy.wait()
    for plane in range(XS):
        leave(plane).wait()


def in_hbm(x):
    return pltpu.with_memory_space_constraint(x, pltpu.HBM)


def body(positions, forces, counts, anchors, helpers):
    bins, _, particles = positions.shape
    count = lax.axis_size("narrow")
    wide = lax.axis_size("wide")
    me = lax.axis_index("narrow")
    block = NZ // count
    own_rows = NY // count
    slabs = 1 + (PATCH + XS - 2) // XS
    slots = slabs * count
    stride = (2 * particles // LANES * bins + 1 + 7) // 8 * 8

    pitch = ((NY + WINDOW) // SPLIT * (SPLIT + 1) + slots - 1) // slots * slots
    folded_rows = 2 * block // LANES * pitch * XS
    parts, folded = pl.pallas_call(
        lambda *refs: gather_kernel(*refs, wide=wide, count=count, slabs=slabs, stride=stride),
        in_specs=[pl.BlockSpec(memory_space=pl.ANY)] * 5,
        out_specs=[pl.BlockSpec(memory_space=pl.ANY), pl.BlockSpec(memory_space=pltpu.VMEM)],
        out_shape=[
            pltpu.VMEM((slots, stride, LANES), jnp.int32),
            pltpu.VMEM((folded_rows, LANES), jnp.float32),
        ],
        scratch_shapes=[
            pltpu.VMEM(positions.shape, jnp.float32),
            pltpu.VMEM(forces.shape, jnp.float32),
            pltpu.VMEM((1, bins), jnp.int32),
            pltpu.VMEM(anchors.shape, jnp.int32),
            pltpu.VMEM((1, bins), jnp.int32),
            pltpu.VMEM((stride, LANES), jnp.int32),
            pltpu.SemaphoreType.DMA((slots,)),
            pltpu.SemaphoreType.DMA((slots,)),
            pltpu.SemaphoreType.DMA,
            pltpu.SemaphoreType.DMA((5,)),
        ],
        compiler_params=pltpu.CompilerParams(
            collective_id=0, has_side_effects=True, vmem_limit_bytes=16 * 1024 * 1024
        ),
        name="gather_particles",
    )(*map(in_hbm, (positions, forces, counts.reshape(1, bins), anchors, helpers.reshape(1, bins))))
    ytab = jnp.asarray(y_tables())
    ztab = jnp.asarray(z_tables(block, count))
    meta = 2 * particles // LANES * bins

    spectrum, load, _ = pl.pallas_call(
        lambda *refs: spectrum_kernel(
            *refs, bins=bins, block=block, count=count, own_rows=own_rows, slabs=slabs
        ),
        in_specs=[pl.BlockSpec(memory_space=pltpu.VMEM)] * 2
        + [pl.BlockSpec(memory_space=pl.ANY)] * 2,
        out_specs=[
            pl.BlockSpec(memory_space=pl.ANY),
            pl.BlockSpec(memory_space=pl.ANY),
            pl.BlockSpec(memory_space=pltpu.VMEM),
        ],
        scratch_shapes=[
            pltpu.VMEM((1, 1), jnp.float32),
            pltpu.SMEM((2 * count,), jnp.float32),
            pltpu.SMEM((slots, LANES), jnp.int32),
            pltpu.VMEM((slots * meta, LANES), jnp.float32),
            pltpu.VMEM((slots * meta, LANES), jnp.float32),
            pltpu.SMEM((slots * bins + 4 * TOGETHER,), jnp.int32),
            pltpu.VMEM(ztab.shape[1:], jnp.bfloat16),
            pltpu.VMEM(ytab.shape, jnp.bfloat16),
            pltpu.VMEM((XS, 2, block, NY), jnp.float32),
            pltpu.SemaphoreType.DMA((4,)),
            pltpu.SemaphoreType.DMA((XS,)),
        ]
        + [pltpu.VMEM((XS * PATCH, particles), jnp.bfloat16)] * (2 * TOGETHER)
        + [pltpu.VMEM((block + WINDOW, particles), jnp.float32)] * (2 * TOGETHER)
        + [pltpu.VMEM((PATCH, particles), jnp.float32)] * (2 * TOGETHER),
        out_shape=[
            jax.ShapeDtypeStruct((2, XS, block, NY), jnp.float32),
            jax.ShapeDtypeStruct((1, 1), jnp.float32),
            pltpu.VMEM((folded_rows, LANES), jnp.float32),
        ],
        input_output_aliases={1: 2},
        compiler_params=pltpu.CompilerParams(vmem_limit_bytes=36 * 1024 * 1024),
        name="spread_and_transform",
    )(
        pltpu.with_memory_space_constraint(parts, pltpu.VMEM),
        pltpu.with_memory_space_constraint(folded, pltpu.VMEM),
        in_hbm(ztab),
        in_hbm(ytab),
    )
    return (spectrum, load)


def solution(mesh):
    return jax.shard_map(
        body,
        mesh=mesh,
        in_specs=(
            P(("wide", "narrow"), None, None),
            P(("wide", "narrow"), None),
            P(("wide", "narrow")),
            P(None, ("wide", "narrow")),
            P(("wide", "narrow"), None),
        ),
        out_specs=(P(None, "wide", "narrow", None), P("wide", "narrow")),
        check_vma=False,
    )
```
